256 devices in a mesh: modes: 4 (over y_hi, core), space: 64 (over x, y_lo, z).
Axes of the slice: x: 4, y: 4 (y_hi: 2, y_lo: 2; y = y_hi * 2 + y_lo), z: 8, core: 2. Of those that a mesh axis runs over, the one named last changes fastest.
Arguments:
- thermal_deviation_iterate: float32 [4, 256, 256], P(None, 'space'), may hold values from -6 to 6
- volumetric_source_term: float32 [4, 256, 256], P(None, 'space'), may hold values from -6 to 6
- node_substance_label: int32 [4, 256, 256], P(None, 'space'), may hold values from 0 to 2
- spectral_table_lookup: int32 [40], P('modes'), may hold values from 0 to 63
- propagation_velocity_table: float32 [64], replicated, may hold values from 0.7 to 1
- specific_heat_table: float32 [64], replicated, may hold values from 0.5 to 2
- collision_frequency_table: float32 [64, 3], replicated, may hold values from 0.08 to 0.4
- ordinate_inclination: float32 [30], replicated, may hold values from 0.05 to 1.52
- ordinate_longitude: float32 [30], replicated, may hold values from -3.140625 to 3.140625
Outputs:
- new_temperature: float32 [4, 256, 256], P(None, 'space', 'modes')
- heat_flux: float32 [3, 4, 256, 256], P(None, None, 'space', 'modes')
The draws below stay inside these ranges and needn't reach their ends.
All inputs are finite; a program needn't handle non-finite values.
Results may differ from the reference program's by a relative error of at most 0.000078.
Values sent between devices are 32-bit elements; how exact they have to be, the bound alone decides.
A program may use at most 64 MiB of HBM per device.

```python
import math
import jax
import jax.numpy as jnp
from jax import lax

SPECTRAL_BINS = 40
HALF_DIR = 30
ANGULAR_ORDINATES = 60
TABLE = 64
LATERAL_NODES_V = 256
SLAB_LAYERS = 4
SWEEPS = 3
CHEB = 16
LATERAL_NODES_U = 256


def with_ends(values, key, least, largest):
    shape = values.shape
    spot = [jax.random.randint(jax.random.fold_in(key, axis), (), 0, shape[axis]) for axis in range(len(shape))]
    values = values.at[tuple(spot)].set(least)
    longest = shape.index(max(shape))
    spot[longest] = (spot[longest] + 1) % shape[longest]
    return values.at[tuple(spot)].set(largest)


def steps_of(rng, extent, pieces, least, largest):
    loudness = 1.0
    for dim, parts in pieces:
        steps = jax.random.uniform(jax.random.fold_in(jax.random.fold_in(rng, 6), dim), (parts,), jnp.float32, least / len(pieces), largest / len(pieces))
        loudness = loudness * jnp.repeat(jnp.exp(steps), extent[dim] // parts).reshape((-1,) + (1,) * (len(extent) - 1 - dim))
    return loudness


def scatter_about(rng, shape, deviation, bound, split=(), held_as=jnp.bfloat16):
    gain = steps_of(rng, shape, split, -0.22, 0.18) if split else 1.0
    drawn = jax.random.normal(rng, shape, jnp.float32) * deviation * gain
    return jnp.minimum(jnp.maximum(drawn, -bound), bound).astype(held_as)


def setup_inputs(seed: int = 0) -> dict:
    streams_of = jax.random.split(jax.random.key(seed), 10)
    thermal_deviation_iterate = scatter_about(streams_of[0], (SLAB_LAYERS, LATERAL_NODES_U, LATERAL_NODES_V), 1.0, 6.0, ((1, 64),), jnp.float32)
    volumetric_source_term = scatter_about(streams_of[1], (SLAB_LAYERS, LATERAL_NODES_U, LATERAL_NODES_V), 1.0, 6.0, ((1, 64),), jnp.float32)
    node_substance_label = with_ends(jax.random.randint(streams_of[2], (SLAB_LAYERS, LATERAL_NODES_U, LATERAL_NODES_V), 0, 3), jax.random.fold_in(streams_of[2], 1), 0, 2).astype(jnp.int32)
    spectral_table_lookup = with_ends(jax.random.randint(streams_of[3], (SPECTRAL_BINS,), 0, TABLE), jax.random.fold_in(streams_of[3], 1), 0, TABLE - 1).astype(jnp.int32)
    propagation_velocity_table = jnp.clip(jax.random.uniform(streams_of[4], (TABLE,), jnp.float32, 0.7, 1.0), 0.7, 1.0)
    specific_heat_table = jnp.clip(jnp.exp(jax.random.uniform(streams_of[5], (TABLE,), jnp.float32, math.log(0.5), math.log(2.0))), 0.5, 2.0)
    collision_frequency_table = jnp.clip(jnp.exp(jax.random.uniform(streams_of[6], (TABLE, 3), jnp.float32, math.log(0.08), math.log(0.4))), 0.08, 0.4)
    ordinate_inclination = jnp.clip(jax.random.uniform(streams_of[7], (HALF_DIR,), jnp.float32, 0.05, 1.52), 0.05, 1.52)
    ordinate_longitude = jnp.clip(jax.random.uniform(streams_of[8], (HALF_DIR,), jnp.float32, -3.140625, 3.140625), -3.140625, 3.140625)
    return dict(thermal_deviation_iterate=thermal_deviation_iterate, volumetric_source_term=volumetric_source_term, node_substance_label=node_substance_label, spectral_table_lookup=spectral_table_lookup, propagation_velocity_table=propagation_velocity_table, specific_heat_table=specific_heat_table, collision_frequency_table=collision_frequency_table, ordinate_inclination=ordinate_inclination, ordinate_longitude=ordinate_longitude)


def directions(ordinate_inclination, ordinate_longitude):
    along_x = jnp.cos(ordinate_inclination)
    along_y = jnp.sin(ordinate_inclination) * jnp.cos(ordinate_longitude)
    along_z = jnp.sin(ordinate_inclination) * jnp.sin(ordinate_longitude)
    return (jnp.concatenate([along_x, -along_x]), jnp.concatenate([along_y, -along_y]),
            jnp.concatenate([along_z, -along_z]))


def diffuse_apply(padded_values, padded_kappa):
    center = padded_values[1:-1, 1:-1, 1:-1]
    kappa_here = padded_kappa[1:-1, 1:-1, 1:-1]
    slices = [(slice(1, -1), slice(None, -2), slice(1, -1)), (slice(1, -1), slice(2, None), slice(1, -1)),
              (slice(1, -1), slice(1, -1), slice(None, -2)), (slice(1, -1), slice(1, -1), slice(2, None)),
              (slice(None, -2), slice(1, -1), slice(1, -1)), (slice(2, None), slice(1, -1), slice(1, -1))]
    total = jnp.zeros_like(center)
    for where in slices:
        total = total + 0.5 * (kappa_here + padded_kappa[where]) * (center - padded_values[where])
    return center + total


def reference(thermal_deviation_iterate, volumetric_source_term, node_substance_label, spectral_table_lookup, propagation_velocity_table, specific_heat_table, collision_frequency_table, ordinate_inclination, ordinate_longitude):
    velocity = propagation_velocity_table[spectral_table_lookup]
    spectral = (jnp.arange(SPECTRAL_BINS).astype(jnp.float32) + 1.0) / SPECTRAL_BINS
    specific_thermal_storage = specific_heat_table[spectral_table_lookup] * spectral
    rates = collision_frequency_table[spectral_table_lookup]
    along_x, along_y, along_z = directions(ordinate_inclination, ordinate_longitude)
    masks = [(node_substance_label == kind).astype(jnp.float32) for kind in range(3)]
    node_collision_frequency = (rates[:, 0, None, None, None] * masks[0] + rates[:, 1, None, None, None] * masks[1]
                 + rates[:, 2, None, None, None] * masks[2])[:, None]
    speed_x = velocity[:, None] * along_x[None, :]
    speed_y = velocity[:, None] * along_y[None, :]
    speed_z = velocity[:, None] * along_z[None, :]

    def expand(coef):
        return coef[:, :, None, None, None]

    abs_sum = jnp.abs(along_x) + jnp.abs(along_y) + jnp.abs(along_z)
    denom = expand(velocity[:, None] * abs_sum[None, :]) + node_collision_frequency
    equilibrium_emission = specific_thermal_storage[:, None, None, None, None] * (node_collision_frequency * thermal_deviation_iterate + volumetric_source_term)
    iteration_bundle = jnp.broadcast_to(specific_thermal_storage[:, None, None, None, None] * thermal_deviation_iterate, (SPECTRAL_BINS, ANGULAR_ORDINATES) + thermal_deviation_iterate.shape)
    for sweep_index in range(SWEEPS):
        xpad = jnp.pad(iteration_bundle, ((0, 0), (0, 0), (0, 0), (1, 1), (0, 0)))
        ypad = jnp.pad(iteration_bundle, ((0, 0), (0, 0), (0, 0), (0, 0), (1, 1)))
        zpad = jnp.pad(iteration_bundle, ((0, 0), (0, 0), (1, 1), (0, 0), (0, 0)))
        xterm = expand(jnp.maximum(speed_x, 0.0)) * xpad[:, :, :, :-2] + expand(jnp.maximum(-speed_x, 0.0)) * xpad[:, :, :, 2:]
        yterm = expand(jnp.maximum(speed_y, 0.0)) * ypad[..., :-2] + expand(jnp.maximum(-speed_y, 0.0)) * ypad[..., 2:]
        zterm = expand(jnp.maximum(speed_z, 0.0)) * zpad[:, :, :-2] + expand(jnp.maximum(-speed_z, 0.0)) * zpad[:, :, 2:]
        iteration_bundle = (xterm + yterm + zterm + equilibrium_emission) / denom
    summed = jnp.sum(iteration_bundle, axis=1)
    numer = jnp.sum(node_collision_frequency[:, 0] * summed, axis=0) / ANGULAR_ORDINATES
    fluxes = [jnp.einsum('fd,fdpxy->pxy', coef, iteration_bundle, precision=lax.Precision.HIGHEST) / ANGULAR_ORDINATES
              for coef in (speed_x, speed_y, speed_z)]
    rate_total = jnp.sum(specific_thermal_storage[:, None] * rates, axis=0)
    cond_total = jnp.sum((specific_thermal_storage * velocity * velocity)[:, None] / (3.0 * rates), axis=0)
    conduct = cond_total / rate_total
    kappa = conduct[0] * masks[0] + conduct[1] * masks[1] + conduct[2] * masks[2]
    cell_total = rate_total[0] * masks[0] + rate_total[1] * masks[1] + rate_total[2] * masks[2]
    hemisphere_ordinates = numer / cell_total
    top = 1.0 + 12.0 * jnp.max(conduct)
    theta = (top + 1.0) / 2.0
    delta = (top - 1.0) / 2.0
    sigma = theta / delta
    padded_kappa = jnp.pad(kappa, 1)
    correction = jnp.zeros_like(hemisphere_ordinates)
    equation_mismatch = hemisphere_ordinates - thermal_deviation_iterate
    direction = equation_mismatch / theta
    rho = 1.0 / sigma
    for cheb_index in range(CHEB):
        correction = correction + direction
        equation_mismatch = equation_mismatch - diffuse_apply(jnp.pad(direction, 1), padded_kappa)
        rho_new = 1.0 / (2.0 * sigma - rho)
        direction = (rho_new * rho) * direction + (2.0 * rho_new / delta) * equation_mismatch
        rho = rho_new
    return hemisphere_ordinates + correction, jnp.stack(fluxes)
```

```python
import functools

import jax
import jax.numpy as jnp
from jax import lax
from jax.experimental import pallas as pl
from jax.experimental.pallas import tpu as pltpu
from jax.sharding import PartitionSpec as P

SPECTRAL_BINS = 40
ORDINATES = 60
CHEB = 16
FT = SPECTRAL_BINS // 8
REACH = 4
HALF_PI = 1.5707964
MESH = pl.DeviceIdType.MESH
OFFSETS = tuple(o for r in range(1, REACH + 1) for o in (r, -r))


def iota(shape, dim):
    return lax.broadcasted_iota(jnp.int32, shape, dim)


def permuted(x, chosen):
    rows = x.shape[0]
    first = x.astype(jnp.bfloat16)
    rest = x - first.astype(jnp.float32)
    second = rest.astype(jnp.bfloat16)
    third = (rest - second.astype(jnp.float32)).astype(jnp.bfloat16)
    stacked = jnp.concatenate([first, second, third], axis=0)
    out = jnp.dot(stacked, chosen, preferred_element_type=jnp.float32)
    return out[:rows] + (out[rows : 2 * rows] + out[2 * rows :])


def ones_where(cond):
    return jnp.where(cond, 1.0, 0.0).astype(jnp.bfloat16)


def kernel(
    n_space, n_modes,
    t_ref, s_ref, l_ref, idx_ref, vel_ref, heat_ref, rates_ref, pol_ref, azi_ref, azs_ref,
    out_t, out_f,
    h_t, h_s, h_l, look, raw, il, dirs, shifted, d_ref, src, srcp, lab, qt, cv, p_ref, g_ref, acc,
    w_int, w_num, w_flux, tables, t_win, l_send, l_recv, nq, n_send, n_recv, fq, f_send, f_recv,
    half_ref, r_send, r_recv, field, coup, cheb_c,
    hs, hr, ls, lr, ws, wr, ns, nr, fs, fr, rs, rr,
):
    m = lax.axis_index("modes")
    s = lax.axis_index("space")
    forward = m < n_modes // 2
    step = jnp.where(forward, 1, -1)

    def peer(j):
        return lax.rem(m + j, n_modes)

    def beside(o):
        return lax.rem(s + o + n_space, n_space)

    barrier = pltpu.get_barrier_semaphore()
    for j in range(1, n_modes):
        pl.semaphore_signal(barrier, inc=1, device_id=(peer(j), s), device_id_type=MESH)
    for o in OFFSETS:
        pl.semaphore_signal(barrier, inc=1, device_id=(m, beside(o)), device_id_type=MESH)

    y0 = 64 * m - 32
    natural = ones_where(iota((256, 128), 0) == iota((256, 128), 1) + y0)
    for z in range(4):
        raw[pl.ds(4 * z, 4), :] = t_ref[z]
        raw[pl.ds(16 + 4 * z, 4), :] = l_ref[z].astype(jnp.float32)
    windows = permuted(raw[0:32, :], natural)
    t_win[...] = windows[0:16]
    l_send[...] = windows[16:32]
    l_recv[REACH] = windows[16:32]
    look[0] = jnp.zeros((1, 128), jnp.int32)
    look[0, :, 0:10] = idx_ref[...]

    pl.semaphore_wait(barrier, n_modes - 1 + len(OFFSETS))

    def remote(source, target, send, recv, device):
        copy = pltpu.make_async_remote_copy(
            src_ref=source, dst_ref=target, send_sem=send, recv_sem=recv,
            device_id=device, device_id_type=MESH,
        )
        copy.start()
        return copy

    down = (m, beside(step))
    halo_copies = [
        remote(t_ref, h_t, hs.at[0], hr.at[0], down),
        remote(s_ref, h_s, hs.at[1], hr.at[1], down),
        remote(l_ref, h_l, hs.at[2], hr.at[2], down),
    ]
    look_copies = [
        remote(look.at[0], look.at[j], ls.at[j - 1], lr.at[j - 1], (peer(j), s))
        for j in range(1, n_modes)
    ]
    window_copies = [
        remote(l_send, l_recv.at[REACH - o], ws.at[i], wr.at[i], (m, beside(o)))
        for i, o in enumerate(OFFSETS)
    ]

    spot = iota((32, 128), 0) == iota((32, 128), 1)

    def column(row_ref):
        row = jnp.concatenate([row_ref[...], jnp.zeros((1, 98), jnp.float32)], axis=1)
        picked = jnp.where(spot, jnp.broadcast_to(row, (32, 128)), 0.0)
        return jnp.broadcast_to(jnp.sum(picked, axis=1, keepdims=True), (32, 128))

    polar, azimuth = column(pol_ref), column(azi_ref)
    sign = jnp.where(forward, 1.0, -1.0)
    u_x = jnp.cos(polar)
    u_y = jnp.sin(polar) * jnp.cos(azimuth)
    u_z = jnp.sin(polar) * jnp.sin(azimuth)
    y_up = jnp.where(jnp.abs(azimuth) < HALF_PI, sign, -sign)
    z_up = jnp.where(azimuth > 0.0, sign, -sign)
    dirs[0, 0:32, :] = u_x
    dirs[1, 0:32, :] = jnp.abs(u_y)
    dirs[2, 0:32, :] = jnp.abs(u_z)
    dirs[3, 0:32, :] = u_x + jnp.abs(u_y) + jnp.abs(u_z)
    dirs[4, 0:32, :] = y_up
    dirs[5, 0:32, :] = z_up
    dirs[6, 0:32, :] = sign * u_x
    dirs[7, 0:32, :] = sign * u_y
    dirs[8, 0:32, :] = sign * u_z

    y_of = 2 * (iota((256, 128), 0) & 127) + (iota((256, 128), 0) >> 7)
    lane = iota((256, 128), 1)
    for tile in range(2):
        w_int[:, tile * 128 : (tile + 1) * 128] = ones_where(iota((256, 128), 0) == 2 * lane + tile)
    for j in range(n_modes):
        w_num[:, j * 128 : (j + 1) * 128] = ones_where(y_of == lane + (64 * peer(j) - 32))
        w_flux[:, j * 128 : (j + 1) * 128] = ones_where((y_of == lane + 64 * peer(j)) & (lane < 64))

    for copy in look_copies:
        copy.wait_recv()
    freq = iota((SPECTRAL_BINS, 128), 0)
    slot = freq // 10
    spread = jnp.zeros((SPECTRAL_BINS, 128), jnp.float32)
    ordinal = jnp.zeros((SPECTRAL_BINS, 128), jnp.float32)
    for j in range(n_modes):
        row = jnp.broadcast_to(look[j].astype(jnp.float32), (SPECTRAL_BINS, 128))
        spread = jnp.where(slot == j, row, spread)
        owner = lax.rem(m + n_modes - j, n_modes)
        ordinal = jnp.where(slot == j, (10 * owner + 1).astype(jnp.float32), ordinal)
    within = freq - 10 * slot
    spectral = (ordinal + within.astype(jnp.float32)) / float(SPECTRAL_BINS)
    index = jnp.sum(
        jnp.where(iota((SPECTRAL_BINS, 128), 1) == within, spread, 0.0), axis=1, keepdims=True
    )
    chosen = iota((SPECTRAL_BINS, 64), 1).astype(jnp.float32) == index
    onehot = jnp.where(chosen, 1.0, 0.0)

    def looked_up(row):
        found = jnp.sum(onehot * row, axis=1, keepdims=True)
        return jnp.broadcast_to(found, (SPECTRAL_BINS, 128))

    velocity = looked_up(vel_ref[...])
    capacity = looked_up(heat_ref[...]) * spectral
    by_kind_of_f = [looked_up(rates_ref[k : k + 1, :]) for k in range(3)]
    kind_lane = iota((SPECTRAL_BINS, 128), 1)
    rate = jnp.where(kind_lane == 0, by_kind_of_f[0], jnp.where(kind_lane == 1, by_kind_of_f[1], by_kind_of_f[2]))
    kinds = iota((1, 128), 1)
    rate_total = jnp.sum(capacity * rate, axis=0, keepdims=True)
    cond = capacity * velocity * velocity / (3.0 * rate)
    cond_total = jnp.sum(cond, axis=0, keepdims=True)
    conduct = cond_total / rate_total
    for k in range(3):
        def splat(row):
            one = jnp.sum(jnp.where(kinds == k, row, 0.0), axis=1, keepdims=True)
            return jnp.broadcast_to(one, (1, 128))
        tables[k] = splat(rate_total)
        tables[3 + k] = splat(conduct)
    per_v = rate / velocity
    cap_v = capacity * velocity
    inv_v = 1.0 / velocity
    for f in range(FT):
        qt[f] = per_v[8 * f : 8 * f + 8]
        cv[f] = cap_v[8 * f : 8 * f + 8]

    for copy in halo_copies:
        copy.wait_recv()
    has = jnp.where(forward, s > 0, s < n_space - 1)
    for k in range(7):
        base = k + 1 if k < 3 else k - 3
        refs = (h_t, h_s, h_l) if k < 3 else (t_ref, s_ref, l_ref)

        def row_of(ref, z):
            return jnp.where(forward, ref[z, base : base + 1, :], ref[z, 3 - base : 4 - base, :])

        for z in range(4):
            t_row = row_of(refs[0], z)
            raw[4 * k + z : 4 * k + z + 1, :] = jnp.where(has, t_row, 0.0) if k < 3 else t_row
            if k > 0:
                at = 4 * (k - 1) + z
                s_row = row_of(refs[1], z)
                raw[32 + at : 33 + at, :] = jnp.where(has, s_row, 0.0) if k < 3 else s_row
                raw[56 + at : 57 + at, :] = row_of(refs[2], z).astype(jnp.float32)
    raw[28:32, :] = jnp.zeros((4, 256), jnp.float32)
    il[...] = permuted(raw[...], w_int[...])

    level = iota((24, 256), 0) & 3
    shifted[0] = il[0:24, :]
    shifted[3] = jnp.where(level == 0, 0.0, il[3:27, :])
    shifted[4] = jnp.where(level == 3, 0.0, il[5:29, :])
    tile_lane = iota((24, 128), 1)
    even, odd = il[4:28, 0:128], il[4:28, 128:256]
    shifted[1, :, 0:128] = jnp.where(tile_lane == 0, 0.0, pltpu.roll(odd, 1, 1))
    shifted[1, :, 128:256] = even
    shifted[2, :, 0:128] = odd
    shifted[2, :, 128:256] = jnp.where(tile_lane == 127, 0.0, pltpu.roll(even, 127, 1))

    for i in range(24):
        for tile in range(2):
            cols = slice(tile * 128, (tile + 1) * 128)
            kind = jnp.broadcast_to(il[56 + i : 57 + i, cols], (8, 128)).astype(jnp.int32)
            lab[i, tile] = kind
            temp = jnp.broadcast_to(il[4 + i : 5 + i, cols], (8, 128))
            heat = jnp.broadcast_to(il[32 + i : 33 + i, cols], (8, 128))
            for f in range(FT):
                q = jnp.take_along_axis(qt[f], kind, axis=1)
                value = q * temp + inv_v[8 * f : 8 * f + 8] * heat
                src[f, i, tile] = value
                if i >= 8:
                    srcp[f, i, tile] = cv[f] * value

    def clear(i, _):
        for which in range(4):
            for tile in range(2):
                acc[which, i, tile] = jnp.zeros((8, 128), jnp.float32)
        return 0

    lax.fori_loop(0, 16, clear, 0)

    lanes8 = iota((8, 128), 1)
    first = lax.rem(m, n_modes // 2) * 15

    def per_direction(j, _):
        d = first + j

        def coef(which):
            return dirs[which, pl.ds(d, 8, stride=0), :]

        def wide(row):
            return row

        def tall(row):
            return jnp.concatenate([row] * 3, axis=0)

        a_x, a_y, a_z, a_sum = coef(0), coef(1), coef(2), coef(3)
        y_pos, z_pos = coef(4) > 0.0, coef(5) > 0.0
        fy, by = jnp.where(y_pos, a_y, 0.0), jnp.where(y_pos, 0.0, a_y)
        fz, bz = jnp.where(z_pos, a_z, 0.0), jnp.where(z_pos, 0.0, a_z)
        for tile in range(2):
            cols = slice(tile * 128, (tile + 1) * 128)
            d_ref[tile, 0:24, :] = (
                tall(a_x) * shifted[0, :, cols]
                + tall(fy) * shifted[1, :, cols]
                + tall(by) * shifted[2, :, cols]
                + tall(fz) * shifted[3, :, cols]
                + tall(bz) * shifted[4, :, cols]
            )
        ahead = jnp.logical_xor(jnp.abs(azs_ref[d]) < HALF_PI, jnp.logical_not(forward))
        turn_0 = jnp.where(ahead, 1, 0)
        turn_1 = jnp.where(ahead, 0, 127)
        wide_x, wide_sum = wide(a_x), wide(a_sum)
        wide_y0 = jnp.where(lanes8 == 0, wide(by), wide(a_y))
        wide_y1 = jnp.where(lanes8 == 127, wide(fy), wide(a_y))
        wide_z, wide_fz, wide_bz = wide(a_z), wide(fz), wide(bz)
        up_mask = wide(coef(5)) > 0.0
        for i in range(16):
            for tile in range(2):
                p_ref[i, tile] = jnp.zeros((8, 128), jnp.float32)
                g_ref[i, tile] = jnp.zeros((8, 128), jnp.float32)

        def gathered(before, now, scale, source):
            c_x, c_y0, c_y1, c_z, c_fz, c_bz = scale
            out = [[None, None] for _ in range(4)]
            for z in range(4):
                turned = (
                    c_y0 * pltpu.roll(now[z][1], turn_0, 1),
                    c_y1 * pltpu.roll(now[z][0], turn_1, 1),
                )
                for tile in range(2):
                    if z == 0:
                        vertical = c_bz * now[1][tile]
                    elif z == 3:
                        vertical = c_fz * now[2][tile]
                    else:
                        vertical = c_z * jnp.where(up_mask, now[z - 1][tile], now[z + 1][tile])
                    out[z][tile] = (
                        (c_x * before[z][tile] + turned[tile]) + (vertical + source(z, tile))
                    )
            return out

        def per_block(f, _):
            weights = 1.0 / (wide_sum + qt[f])
            scale = (wide_x, wide_y0, wide_y1, wide_z, wide_fz, wide_bz)
            scaled = tuple(cv[f] * c for c in scale)
            g1_before = g2_before = None
            for k in range(6):
                rows = [4 * k + z for z in range(4)]
                inv = [[jnp.take_along_axis(weights, lab[r, t], axis=1) for t in range(2)] for r in rows]
                g1 = [
                    [
                        inv[z][t]
                        * (d_ref[t, pl.ds(rows[z], 8, stride=0), :] + src[f, rows[z], t])
                        for t in range(2)
                    ]
                    for z in range(4)
                ]
                g2 = None
                if k >= 1:
                    total = gathered(g1_before, g1, scale, lambda z, t: src[f, rows[z], t])
                    g2 = [[inv[z][t] * total[z][t] for t in range(2)] for z in range(4)]
                if k >= 2:
                    total = gathered(g2_before, g2, scaled, lambda z, t: srcp[f, rows[z], t])
                    for z in range(4):
                        i = 4 * (k - 2) + z
                        for t in range(2):
                            p_ref[i, t] += total[z][t]
                            g_ref[i, t] += inv[z][t] * total[z][t]
                g1_before, g2_before = g1, g2
            return 0

        lax.fori_loop(0, FT, per_block, 0)
        v_x, v_y, v_z = wide(coef(6)), wide(coef(7)), wide(coef(8))
        for i in range(16):
            for t in range(2):
                flow = g_ref[i, t]
                acc[0, i, t] += p_ref[i, t] - wide_sum * flow
                acc[1, i, t] += v_x * flow
                acc[2, i, t] += v_y * flow
                acc[3, i, t] += v_z * flow
        return 0

    lax.fori_loop(0, 15, per_direction, 0)

    def summed(which, target, base):
        for z in range(4):
            for t in range(2):
                found = [jnp.sum(acc[which, 4 * k + z, t], axis=0, keepdims=True) for k in range(4)]
                for x in range(4):
                    at = base + 4 * z + x
                    row = jnp.where(forward, found[x], found[3 - x])
                    target[at : at + 1, t * 128 : (t + 1) * 128] = row

    summed(0, nq, 0)
    moved = permuted(nq[...], w_num[...])
    n_recv[0] = moved[:, 0:128]
    for j in range(1, n_modes):
        n_send[j - 1] = moved[:, j * 128 : (j + 1) * 128]
    n_copies = [
        remote(n_send.at[j - 1], n_recv.at[j], ns.at[j - 1], nr.at[j - 1], (peer(j), s))
        for j in range(1, n_modes)
    ]
    for i in range(3):
        summed(1 + i, fq, 16 * i)
    moved = permuted(fq[...], w_flux[...])
    for j in range(n_modes):
        part = moved[:, j * 128 : (j + 1) * 128]
        packed = part[0:24] + pltpu.roll(part[24:48], 64, 1)
        if j == 0:
            f_recv[0] = packed
        else:
            f_send[j - 1] = packed
    f_copies = [
        remote(f_send.at[j - 1], f_recv.at[j], fs.at[j - 1], fr.at[j - 1], (peer(j), s))
        for j in range(1, n_modes)
    ]

    for copy in window_copies:
        copy.wait_recv()
    for b in range(2 * REACH + 1):
        for z in range(4):
            field[z, 4 * b : 4 * b + 4, :] = l_recv[b, 4 * z : 4 * z + 4, :]
    rows = 4 * (2 * REACH + 1)
    padded = rows + 4
    for z in range(4):
        field[z, rows:padded, :] = jnp.zeros((4, 128), jnp.float32)
    x_of = iota((padded, 128), 0) + 4 * (s - REACH)
    y_of_lane = iota((padded, 128), 1) + y0
    inside = (
        (x_of >= 0) & (x_of < 4 * n_space) & (iota((padded, 128), 0) < rows)
        & (y_of_lane >= 0) & (y_of_lane < 256)
    )

    def by_kind(label, base):
        return jnp.where(label == 0.0, tables[base], jnp.where(label == 1.0, tables[base + 1], tables[base + 2]))

    kappa = [jnp.where(inside, by_kind(field[z], 3), 0.0) for z in range(4)]

    def link(here, there):
        mean = 0.5 * (here + there)
        return jnp.where(here > 0.0, mean, 0.0), jnp.where((here > 0.0) & (there > 0.0), mean, 0.0)

    for z in range(4):
        here = kappa[z]
        none = jnp.zeros_like(here)
        around = [
            pltpu.roll(here, 1, 0), pltpu.roll(here, padded - 1, 0),
            pltpu.roll(here, 1, 1), pltpu.roll(here, 127, 1),
            kappa[z - 1] if z > 0 else none, kappa[z + 1] if z < 3 else none,
        ]
        diagonal = jnp.full_like(here, 1.0)
        for which, there in enumerate(around):
            whole, joint = link(here, there)
            diagonal = diagonal + whole
            coup[which, z] = joint
        coup[6, z] = diagonal

    top = 1.0 + 12.0 * jnp.maximum(jnp.maximum(tables[3], tables[4]), tables[5])
    theta = (top + 1.0) / 2.0
    delta = (top - 1.0) / 2.0
    sigma = theta / delta
    rho = 1.0 / sigma
    for k in range(CHEB - 1):
        rho_new = 1.0 / (2.0 * sigma - rho)
        cheb_c[k] = rho_new * rho
        cheb_c[CHEB + k] = 2.0 * rho_new / delta
        rho = rho_new

    for copy in n_copies:
        copy.wait_recv()
    numer = (n_recv[0] + n_recv[1]) + (n_recv[2] + n_recv[3])
    here = l_recv[REACH]
    half = numer / (float(ORDINATES) * by_kind(here, 0))
    mismatch = half - t_win[...]
    half_ref[...] = half
    r_send[...] = mismatch
    r_recv[REACH] = mismatch
    r_copies = [
        remote(r_send, r_recv.at[REACH - o], rs.at[i], rr.at[i], (m, beside(o)))
        for i, o in reversed(tuple(enumerate(OFFSETS)))
    ]

    for copy in f_copies:
        copy.wait_recv()
    flux = ((f_recv[0] + f_recv[1]) + (f_recv[2] + f_recv[3])) / float(ORDINATES)
    for i in range(3):
        for z in range(4):
            at = 16 * i + 4 * z
            out_f[i, z] = flux[at : at + 4, 0:64] if at < 24 else flux[at - 24 : at - 20, 64:128]

    for copy in r_copies:
        copy.wait_recv()
    for b in range(2 * REACH + 1):
        for z in range(4):
            field[z, 4 * b : 4 * b + 4, :] = r_recv[b, 4 * z : 4 * z + 4, :]
    mid = 4 * REACH
    start_r = [jnp.where(inside, field[z], 0.0) for z in range(4)]
    start_d = [r / theta for r in start_r]
    start_c = [d[mid : mid + 8] for d in start_d]

    def advance(k, carry):
        resid, direction, total = carry
        c_1, c_2 = cheb_c[k], cheb_c[CHEB + k]
        new_r, new_d, new_t = [], [], []
        for z in range(4):
            d = direction[z]
            applied = coup[6, z] * d
            applied = applied - coup[0, z] * pltpu.roll(d, 1, 0)
            applied = applied - coup[1, z] * pltpu.roll(d, padded - 1, 0)
            applied = applied - coup[2, z] * pltpu.roll(d, 1, 1)
            applied = applied - coup[3, z] * pltpu.roll(d, 127, 1)
            if z > 0:
                applied = applied - coup[4, z] * direction[z - 1]
            if z < 3:
                applied = applied - coup[5, z] * direction[z + 1]
            r = resid[z] - applied
            after = c_1 * d + c_2 * r
            new_r.append(r)
            new_d.append(after)
            new_t.append(total[z] + after[mid : mid + 8])
        return new_r, new_d, new_t

    _, _, correction = lax.fori_loop(0, CHEB - 1, advance, (start_r, start_d, start_c))
    for z in range(4):
        whole = half_ref[4 * z : 4 * z + 4, :] + correction[z][0:4]
        out_t[z] = pltpu.roll(whole, 96, 1)[:, 0:64]

    for copy in halo_copies + look_copies + window_copies + n_copies + f_copies + r_copies:
        copy.wait_send()


def solution(mesh):
    n_space, n_modes = mesh.shape["space"], mesh.shape["modes"]
    f32, i32 = jnp.float32, jnp.int32
    vmem = pl.BlockSpec(memory_space=pltpu.VMEM)
    dma = pltpu.SemaphoreType.DMA
    blocks = 2 * REACH + 1
    padded = 4 * blocks + 4

    def on_device(temp, source, label, lookup, vel, heat, rates, polar, azimuth):
        scratch = [
            pltpu.VMEM((4, 4, 256), f32), pltpu.VMEM((4, 4, 256), f32), pltpu.VMEM((4, 4, 256), i32),
            pltpu.VMEM((4, 1, 128), i32),
            pltpu.VMEM((80, 256), f32), pltpu.VMEM((80, 256), f32),
            pltpu.VMEM((9, 40, 128), f32), pltpu.VMEM((5, 24, 256), f32), pltpu.VMEM((2, 24 + 8, 128), f32),
            pltpu.VMEM((FT, 24, 2, 8, 128), f32), pltpu.VMEM((FT, 24, 2, 8, 128), f32),
            pltpu.VMEM((24, 2, 8, 128), i32),
            pltpu.VMEM((FT, 8, 128), f32), pltpu.VMEM((FT, 8, 128), f32),
            pltpu.VMEM((16, 2, 8, 128), f32), pltpu.VMEM((16, 2, 8, 128), f32),
            pltpu.VMEM((4, 16, 2, 8, 128), f32),
            pltpu.VMEM((256, 256), jnp.bfloat16),
            pltpu.VMEM((256, 128 * n_modes), jnp.bfloat16), pltpu.VMEM((256, 128 * n_modes), jnp.bfloat16),
            pltpu.VMEM((6, 1, 128), f32),
            pltpu.VMEM((16, 128), f32), pltpu.VMEM((16, 128), f32), pltpu.VMEM((blocks, 16, 128), f32),
            pltpu.VMEM((16, 256), f32), pltpu.VMEM((n_modes - 1, 16, 128), f32), pltpu.VMEM((n_modes, 16, 128), f32),
            pltpu.VMEM((48, 256), f32), pltpu.VMEM((n_modes - 1, 24, 128), f32), pltpu.VMEM((n_modes, 24, 128), f32),
            pltpu.VMEM((16, 128), f32), pltpu.VMEM((16, 128), f32), pltpu.VMEM((blocks, 16, 128), f32),
            pltpu.VMEM((4, padded, 128), f32), pltpu.VMEM((7, 4, padded, 128), f32),
            pltpu.VMEM((2 * CHEB, 1, 128), f32),
            dma((3,)), dma((3,)), dma((n_modes - 1,)), dma((n_modes - 1,)),
            dma((2 * REACH,)), dma((2 * REACH,)), dma((n_modes - 1,)), dma((n_modes - 1,)),
            dma((n_modes - 1,)), dma((n_modes - 1,)), dma((2 * REACH,)), dma((2 * REACH,)),
        ]
        call = pl.pallas_call(
            functools.partial(kernel, n_space, n_modes),
            out_shape=(
                jax.ShapeDtypeStruct((4, 4, 64), f32),
                jax.ShapeDtypeStruct((3, 4, 4, 64), f32),
            ),
            in_specs=[vmem] * 9 + [pl.BlockSpec(memory_space=pltpu.SMEM)],
            out_specs=(vmem, vmem),
            scratch_shapes=scratch,
            compiler_params=pltpu.CompilerParams(collective_id=0, has_side_effects=True),
        )
        return call(
            temp, source, label, lookup[None], vel[None], heat[None], rates.T,
            polar[None], azimuth[None], azimuth,
        )

    rows = P(None, "space", None)
    return jax.shard_map(
        on_device,
        mesh=mesh,
        in_specs=(rows, rows, rows, P("modes"), P(), P(), P(), P(), P()),
        out_specs=(P(None, "space", "modes"), P(None, None, "space", "modes")),
        check_vma=False,
    )
```

```python
import functools

import jax
import jax.numpy as jnp
from jax import lax
from jax.experimental import pallas as pl
from jax.experimental.pallas import tpu as pltpu
from jax.sharding import PartitionSpec as P

SPECTRAL_BINS = 40
ORDINATES = 60
CHEB = 16
FT = SPECTRAL_BINS // 8
REACH = 4
HALF_PI = 1.5707964
MESH = pl.DeviceIdType.MESH
OFFSETS = tuple(o for r in range(1, REACH + 1) for o in (r, -r))


def iota(shape, dim):
    return lax.broadcasted_iota(jnp.int32, shape, dim)


def permuted(x, chosen):
    rows = x.shape[0]
    first = x.astype(jnp.bfloat16)
    rest = x - first.astype(jnp.float32)
    second = rest.astype(jnp.bfloat16)
    third = (rest - second.astype(jnp.float32)).astype(jnp.bfloat16)
    stacked = jnp.concatenate([first, second, third], axis=0)
    out = jnp.dot(stacked, chosen, preferred_element_type=jnp.float32)
    return out[:rows] + (out[rows : 2 * rows] + out[2 * rows :])


def lookup(table, kind):
    return jnp.take_along_axis(
        table, kind, axis=1, mode="promise_in_bounds", wrap_negative_indices=False
    )


def ones_where(cond):
    return jnp.where(cond, 1.0, 0.0).astype(jnp.bfloat16)


def kernel(
    n_space, n_modes,
    t_ref, s_ref, l_ref, idx_ref, vel_ref, heat_ref, rates_ref, pol_ref, azi_ref, azs_ref,
    out_t, out_f,
    h_t, h_s, h_l, look, raw, il, dirs, shifted, d_ref, cells, lab, q_of, cv, p_ref, g_ref, acc,
    w_int, w_num, w_flux, tables, t_win, l_send, l_recv, nq, n_send, n_recv, fq, f_send, f_recv,
    half_ref, r_send, r_recv, field, coup, cheb_c,
    hs, hr, ls, lr, ws, wr, ns, nr, fs, fr, rs, rr,
):
    m = lax.axis_index("modes")
    s = lax.axis_index("space")
    forward = m < n_modes // 2
    step = jnp.where(forward, 1, -1)

    def peer(j):
        return lax.rem(m + j, n_modes)

    def beside(o):
        return lax.rem(s + o + n_space, n_space)

    barrier = pltpu.get_barrier_semaphore()
    for j in range(1, n_modes):
        pl.semaphore_signal(barrier, inc=1, device_id=(peer(j), s), device_id_type=MESH)
    for o in OFFSETS:
        pl.semaphore_signal(barrier, inc=1, device_id=(m, beside(o)), device_id_type=MESH)

    y0 = 64 * m - 32
    natural = ones_where(iota((256, 128), 0) == iota((256, 128), 1) + y0)
    for z in range(4):
        raw[pl.ds(4 * z, 4), :] = t_ref[z]
        raw[pl.ds(16 + 4 * z, 4), :] = l_ref[z].astype(jnp.float32)
    windows = permuted(raw[0:32, :], natural)
    t_win[...] = windows[0:16]
    l_send[...] = windows[16:32]
    l_recv[REACH] = windows[16:32]
    look[0] = jnp.zeros((1, 128), jnp.int32)
    look[0, :, 0:10] = idx_ref[...]

    spot = iota((32, 128), 0) == iota((32, 128), 1)

    def column(row_ref):
        row = jnp.concatenate([row_ref[...], jnp.zeros((1, 98), jnp.float32)], axis=1)
        picked = jnp.where(spot, jnp.broadcast_to(row, (32, 128)), 0.0)
        return jnp.broadcast_to(jnp.sum(picked, axis=1, keepdims=True), (32, 128))

    polar, azimuth = column(pol_ref), column(azi_ref)
    sign = jnp.where(forward, 1.0, -1.0)
    u_x = jnp.cos(polar)
    u_y = jnp.sin(polar) * jnp.cos(azimuth)
    u_z = jnp.sin(polar) * jnp.sin(azimuth)
    y_up = jnp.where(jnp.abs(azimuth) < HALF_PI, sign, -sign)
    z_up = jnp.where(azimuth > 0.0, sign, -sign)
    dirs[0, 0:32, :] = u_x
    dirs[1, 0:32, :] = jnp.abs(u_y)
    dirs[2, 0:32, :] = jnp.abs(u_z)
    dirs[3, 0:32, :] = u_x + jnp.abs(u_y) + jnp.abs(u_z)
    dirs[4, 0:32, :] = y_up
    dirs[5, 0:32, :] = z_up
    dirs[6, 0:32, :] = jnp.abs(u_y) / u_x
    dirs[7, 0:32, :] = jnp.abs(u_z) / u_x
    dirs[8, 0:32, :] = (u_x + jnp.abs(u_y) + jnp.abs(u_z)) / u_x
    dirs[9, 0:32, :] = sign * u_y / u_x
    dirs[10, 0:32, :] = sign * u_z / u_x

    y_of = 2 * (iota((256, 128), 0) & 127) + (iota((256, 128), 0) >> 7)
    lane = iota((256, 128), 1)
    for tile in range(2):
        w_int[:, tile * 128 : (tile + 1) * 128] = ones_where(iota((256, 128), 0) == 2 * lane + tile)
    for j in range(n_modes):
        w_num[:, j * 128 : (j + 1) * 128] = ones_where(y_of == lane + (64 * peer(j) - 32))
        w_flux[:, j * 128 : (j + 1) * 128] = ones_where((y_of == lane + 64 * peer(j)) & (lane < 64))

    def clear(j, _):
        for i in range(32):
            p_ref[j, i] = jnp.zeros((8, 128), jnp.float32)
            g_ref[j, i] = jnp.zeros((8, 128), jnp.float32)
        return 0

    lax.fori_loop(0, 16, clear, 0)
    for i in range(32):
        acc[0, i] = jnp.zeros((8, 128), jnp.float32)

    pl.semaphore_wait(barrier, n_modes - 1 + len(OFFSETS))

    def remote(source, target, send, recv, device):
        copy = pltpu.make_async_remote_copy(
            src_ref=source, dst_ref=target, send_sem=send, recv_sem=recv,
            device_id=device, device_id_type=MESH,
        )
        copy.start()
        return copy

    down = (m, beside(step))
    halo_copies = [
        remote(t_ref, h_t, hs.at[0], hr.at[0], down),
        remote(s_ref, h_s, hs.at[1], hr.at[1], down),
        remote(l_ref, h_l, hs.at[2], hr.at[2], down),
    ]
    look_copies = [
        remote(look.at[0], look.at[j], ls.at[j - 1], lr.at[j - 1], (peer(j), s))
        for j in range(1, n_modes)
    ]
    window_copies = [
        remote(l_send, l_recv.at[REACH - o], ws.at[i], wr.at[i], (m, beside(o)))
        for i, o in enumerate(OFFSETS)
    ]

    for copy in look_copies:
        copy.wait_recv()
    freq = iota((SPECTRAL_BINS, 128), 0)
    slot = freq // 10
    spread = jnp.zeros((SPECTRAL_BINS, 128), jnp.float32)
    ordinal = jnp.zeros((SPECTRAL_BINS, 128), jnp.float32)
    for j in range(n_modes):
        row = jnp.broadcast_to(look[j].astype(jnp.float32), (SPECTRAL_BINS, 128))
        spread = jnp.where(slot == j, row, spread)
        owner = lax.rem(m + n_modes - j, n_modes)
        ordinal = jnp.where(slot == j, (10 * owner + 1).astype(jnp.float32), ordinal)
    within = freq - 10 * slot
    spectral = (ordinal + within.astype(jnp.float32)) / float(SPECTRAL_BINS)
    index = jnp.sum(
        jnp.where(iota((SPECTRAL_BINS, 128), 1) == within, spread, 0.0), axis=1, keepdims=True
    )
    chosen = iota((SPECTRAL_BINS, 64), 1).astype(jnp.float32) == index
    onehot = jnp.where(chosen, 1.0, 0.0)

    def looked_up(row):
        found = jnp.sum(onehot * row, axis=1, keepdims=True)
        return jnp.broadcast_to(found, (SPECTRAL_BINS, 128))

    velocity = looked_up(vel_ref[...])
    capacity = looked_up(heat_ref[...]) * spectral
    by_kind_of_f = [looked_up(rates_ref[k : k + 1, :]) for k in range(3)]
    kind_lane = lax.rem(iota((SPECTRAL_BINS, 128), 1), 3)
    rate = jnp.where(kind_lane == 0, by_kind_of_f[0], jnp.where(kind_lane == 1, by_kind_of_f[1], by_kind_of_f[2]))
    kinds = iota((1, 128), 1)
    rate_total = jnp.sum(capacity * rate, axis=0, keepdims=True)
    cond = capacity * velocity * velocity / (3.0 * rate)
    cond_total = jnp.sum(cond, axis=0, keepdims=True)
    conduct = cond_total / rate_total
    for k in range(3):
        def splat(row):
            one = jnp.sum(jnp.where(kinds == k, row, 0.0), axis=1, keepdims=True)
            return jnp.broadcast_to(one, (1, 128))
        tables[k] = splat(rate_total)
        tables[3 + k] = splat(conduct)
    cap_v = capacity * velocity
    inv_v = 1.0 / velocity
    for f in range(FT):
        for kind in range(3):
            q_of[3 * f + kind] = (by_kind_of_f[kind] / velocity)[8 * f : 8 * f + 8]
        cv[f] = cap_v[8 * f : 8 * f + 8]

    def row_of(ref, base, z):
        return jnp.where(forward, ref[z, base : base + 1, :], ref[z, 3 - base : 4 - base, :])

    def fill_cells(i):
        for tile in range(2):
            cols = slice(tile * 128, (tile + 1) * 128)
            at = 2 * i + tile
            kind = jnp.broadcast_to(il[56 + i : 57 + i, cols], (8, 128)).astype(jnp.int32)
            lab[at] = kind
            is_0, is_1 = kind == 0, kind == 1
            temp = jnp.broadcast_to(il[4 + i : 5 + i, cols], (8, 128))
            heat = jnp.broadcast_to(il[32 + i : 33 + i, cols], (8, 128))
            for f in range(FT):
                q = jnp.where(is_0, q_of[3 * f], jnp.where(is_1, q_of[3 * f + 1], q_of[3 * f + 2]))
                value = q * temp + inv_v[8 * f : 8 * f + 8] * heat
                cells[f, at] = value
                if i >= 8:
                    cells[f, 48 + at - 16] = cv[f] * value

    for k in range(4):
        for z in range(4):
            at = 4 * k + z
            raw[at : at + 1, :] = row_of(t_ref, k, z)
            raw[16 + at : 17 + at, :] = row_of(s_ref, k, z)
            raw[32 + at : 33 + at, :] = row_of(l_ref, k, z).astype(jnp.float32)
    turned = permuted(raw[0:48, :], w_int[...])
    il[12:28, :] = turned[0:16]
    il[40:56, :] = turned[16:32]
    il[64:80, :] = turned[32:48]
    il[28:32, :] = jnp.zeros((4, 256), jnp.float32)
    for i in range(8, 24):
        fill_cells(i)

    for copy in halo_copies:
        copy.wait_recv()
    has = jnp.where(forward, s > 0, s < n_space - 1)
    raw[28:32, :] = jnp.zeros((4, 256), jnp.float32)
    for k in range(3):
        for z in range(4):
            at = 4 * k + z
            raw[at : at + 1, :] = jnp.where(has, row_of(h_t, k + 1, z), 0.0)
            if k > 0:
                raw[8 + at : 9 + at, :] = jnp.where(has, row_of(h_s, k + 1, z), 0.0)
                raw[16 + at : 17 + at, :] = row_of(h_l, k + 1, z).astype(jnp.float32)
    turned = permuted(raw[0:32, :], w_int[...])
    il[0:12, :] = turned[0:12]
    il[32:40, :] = turned[12:20]
    il[56:64, :] = turned[20:28]
    for i in range(8):
        fill_cells(i)

    level = iota((24, 256), 0) & 3
    shifted[0] = il[0:24, :]
    shifted[3] = jnp.where(level == 0, 0.0, il[3:27, :])
    shifted[4] = jnp.where(level == 3, 0.0, il[5:29, :])
    tile_lane = iota((24, 128), 1)
    even, odd = il[4:28, 0:128], il[4:28, 128:256]
    shifted[1, :, 0:128] = jnp.where(tile_lane == 0, 0.0, pltpu.roll(odd, 1, 1))
    shifted[1, :, 128:256] = even
    shifted[2, :, 0:128] = odd
    shifted[2, :, 128:256] = jnp.where(tile_lane == 127, 0.0, pltpu.roll(even, 127, 1))

    lanes8 = iota((8, 128), 1)
    first = lax.rem(m, n_modes // 2) * 15

    def look(j):
        total = dirs[3, pl.ds(first + j, 8, stride=0), :]
        slope = dirs[0, pl.ds(first + j, 8, stride=0), :]
        weights = [[slope / (total + q_of[3 * f + kind]) for kind in range(3)] for f in range(FT)]
        for at in range(48):
            kind = lab[at]
            is_0, is_1 = kind == 0, kind == 1
            for f in range(FT):
                w = weights[f]
                cells[f, 80 + at] = jnp.where(is_0, w[0], jnp.where(is_1, w[1], w[2]))

    def upwind_order(j):
        angle = azs_ref[first + j]
        ahead = jnp.logical_xor(jnp.abs(angle) < HALF_PI, jnp.logical_not(forward))
        up = jnp.logical_xor(angle > 0.0, jnp.logical_not(forward))
        levels = [jnp.where(up, z, 3 - z) for z in range(4)]
        tiles = [jnp.where(ahead, q, 1 - q) for q in range(2)]
        return levels, tiles, ahead

    def stored_at(j):
        levels, tiles, _ = upwind_order(j)
        return [[2 * levels[z] + tiles[t] for t in range(2)] for z in range(4)]

    def numerator(j):
        held = jnp.where(j < 0, 15, j)
        at = jnp.maximum(j, 0)
        ratio = dirs[8, pl.ds(first + at, 8, stride=0), :]
        place = stored_at(at)
        for k in range(4):
            for z in range(4):
                for t in range(2):
                    cell = 8 * k + place[z][t]
                    acc[0, 8 * k + 2 * z + t] += p_ref[held, cell] - ratio * g_ref[held, cell]

    def per_direction(j, _):
        d = first + j
        look(j)
        numerator(j - 1)

        def coef(which):
            return dirs[which, pl.ds(d, 8, stride=0), :]

        def tall(row):
            return jnp.concatenate([row] * 3, axis=0)

        a_x, a_y, a_z = coef(0), coef(1), coef(2)
        y_pos, z_pos = coef(4) > 0.0, coef(5) > 0.0
        fy, by = jnp.where(y_pos, a_y, 0.0), jnp.where(y_pos, 0.0, a_y)
        fz, bz = jnp.where(z_pos, a_z, 0.0), jnp.where(z_pos, 0.0, a_z)
        for tile in range(2):
            cols = slice(tile * 128, (tile + 1) * 128)
            d_ref[tile, 0:24, :] = (
                tall(a_x) * shifted[0, :, cols]
                + tall(fy) * shifted[1, :, cols]
                + tall(by) * shifted[2, :, cols]
                + tall(fz) * shifted[3, :, cols]
                + tall(bz) * shifted[4, :, cols]
            )
        levels, tiles, ahead = upwind_order(j)
        turn = jnp.where(ahead, 1, 127)
        place = [[2 * levels[z] + tiles[q] for q in range(2)] for z in range(4)]
        r_y, r_z = coef(6), coef(7)
        r_edge = jnp.where(lanes8 == jnp.where(ahead, 0, 127), 0.0, r_y)

        def gathered(before, now, scale, source):
            c_x, c_y, c_edge, c_z = scale
            out = [[None, None] for _ in range(4)]
            for z in range(4):
                along = (c_edge * pltpu.roll(now[z][1], turn, 1), c_y * now[z][0])
                for q in range(2):
                    behind = before[z][q] if c_x is None else c_x * before[z][q]
                    total = (behind + along[q]) + source(z, q)
                    out[z][q] = total + c_z * now[z - 1][q] if z > 0 else total
            return out

        both = range(2)
        scale = (None, r_y, r_edge, r_z)

        def per_block(f, _):
            scaled = (cv[f], cv[f] * r_y, cv[f] * r_edge, cv[f] * r_z)
            h1_before = h2_before = None
            for k in range(6):
                inv = [[cells[f, 80 + 8 * k + place[z][q]] for q in both] for z in range(4)]
                here = [[cells[f, 8 * k + place[z][q]] for q in both] for z in range(4)]
                h1 = [
                    [
                        inv[z][q]
                        * (d_ref[tiles[q], pl.ds(4 * k + levels[z], 8, stride=0), :] + here[z][q])
                        for q in both
                    ]
                    for z in range(4)
                ]
                h2 = None
                if k >= 1:
                    total = gathered(h1_before, h1, scale, lambda z, q: here[z][q])
                    h2 = [[inv[z][q] * total[z][q] for q in both] for z in range(4)]
                if k >= 2:
                    total = gathered(
                        h2_before, h2, scaled, lambda z, q: cells[f, 48 + 8 * (k - 2) + place[z][q]]
                    )
                    for z in range(4):
                        for q in both:
                            i = 8 * (k - 2) + 2 * z + q
                            p_ref[j, i] += total[z][q]
                            g_ref[j, i] += inv[z][q] * total[z][q]
                h1_before, h2_before = h1, h2
            return 0

        lax.fori_loop(0, FT, per_block, 0)
        return 0

    lax.fori_loop(0, 15, per_direction, 0)

    numerator(14)
    zero = jnp.zeros((8, 128), jnp.float32)

    def fluxes():
        for k in range(4):
            def flux_of(j, totals):
                v_y = dirs[9, pl.ds(first + j, 8, stride=0), :]
                v_z = dirs[10, pl.ds(first + j, 8, stride=0), :]
                place = stored_at(j)
                out = []
                for z in range(4):
                    for t in range(2):
                        flow = g_ref[j, 8 * k + place[z][t]]
                        n = len(out)
                        out += [totals[n] + flow, totals[n + 1] + v_y * flow, totals[n + 2] + v_z * flow]
                return out

            found = lax.fori_loop(0, 15, flux_of, [zero] * 24)
            for n in range(8):
                acc[1, 8 * k + n] = sign * found[3 * n]
                acc[2, 8 * k + n] = found[3 * n + 1]
                acc[3, 8 * k + n] = found[3 * n + 2]

    def summed(which, target, base):
        for z in range(4):
            for t in range(2):
                found = [jnp.sum(acc[which, 8 * k + 2 * z + t], axis=0, keepdims=True) for k in range(4)]
                for x in range(4):
                    at = base + 4 * z + x
                    row = jnp.where(forward, found[x], found[3 - x])
                    target[at : at + 1, t * 128 : (t + 1) * 128] = row

    summed(0, nq, 0)
    moved = permuted(nq[...], w_num[...])
    n_recv[0] = moved[:, 0:128]
    for j in range(1, n_modes):
        n_send[j - 1] = moved[:, j * 128 : (j + 1) * 128]
    n_copies = [
        remote(n_send.at[j - 1], n_recv.at[j], ns.at[j - 1], nr.at[j - 1], (peer(j), s))
        for j in range(1, n_modes)
    ]
    for copy in window_copies:
        copy.wait_recv()
    for b in range(2 * REACH + 1):
        for z in range(4):
            field[z, 4 * b : 4 * b + 4, :] = l_recv[b, 4 * z : 4 * z + 4, :]
    rows = 4 * (2 * REACH + 1)
    padded = rows + 4
    for z in range(4):
        field[z, rows:padded, :] = jnp.zeros((4, 128), jnp.float32)
    x_of = iota((padded, 128), 0) + 4 * (s - REACH)
    y_of_lane = iota((padded, 128), 1) + y0
    inside = (
        (x_of >= 0) & (x_of < 4 * n_space) & (iota((padded, 128), 0) < rows)
        & (y_of_lane >= 0) & (y_of_lane < 256)
    )

    def by_kind(label, base):
        return jnp.where(label == 0.0, tables[base], jnp.where(label == 1.0, tables[base + 1], tables[base + 2]))

    kappa = [jnp.where(inside, by_kind(field[z], 3), 0.0) for z in range(4)]

    def link(here, there):
        mean = 0.5 * (here + there)
        return jnp.where(here > 0.0, mean, 0.0), jnp.where((here > 0.0) & (there > 0.0), mean, 0.0)

    for z in range(4):
        here = kappa[z]
        none = jnp.zeros_like(here)
        around = [
            pltpu.roll(here, 1, 0), pltpu.roll(here, padded - 1, 0),
            pltpu.roll(here, 1, 1), pltpu.roll(here, 127, 1),
            kappa[z - 1] if z > 0 else none, kappa[z + 1] if z < 3 else none,
        ]
        diagonal = jnp.full_like(here, 1.0)
        for which, there in enumerate(around):
            whole, joint = link(here, there)
            diagonal = diagonal + whole
            coup[which, z] = joint
        coup[6, z] = diagonal

    top = 1.0 + 12.0 * jnp.maximum(jnp.maximum(tables[3], tables[4]), tables[5])
    theta = (top + 1.0) / 2.0
    delta = (top - 1.0) / 2.0
    sigma = theta / delta
    rho = 1.0 / sigma
    for k in range(CHEB - 1):
        rho_new = 1.0 / (2.0 * sigma - rho)
        cheb_c[k] = rho_new * rho
        cheb_c[CHEB + k] = 2.0 * rho_new / delta
        rho = rho_new

    for copy in n_copies:
        copy.wait_recv()
    numer = (n_recv[0] + n_recv[1]) + (n_recv[2] + n_recv[3])
    here = l_recv[REACH]
    half = numer / (float(ORDINATES) * by_kind(here, 0))
    mismatch = half - t_win[...]
    half_ref[...] = half
    r_send[...] = mismatch
    r_recv[REACH] = mismatch
    r_copies = [
        remote(r_send, r_recv.at[REACH - o], rs.at[i], rr.at[i], (m, beside(o)))
        for i, o in reversed(tuple(enumerate(OFFSETS)))
    ]

    fluxes()
    for i in range(3):
        summed(1 + i, fq, 16 * i)
    moved = permuted(fq[...], w_flux[...])
    for j in range(n_modes):
        part = moved[:, j * 128 : (j + 1) * 128]
        packed = part[0:24] + pltpu.roll(part[24:48], 64, 1)
        if j == 0:
            f_recv[0] = packed
        else:
            f_send[j - 1] = packed
    f_copies = [
        remote(f_send.at[j - 1], f_recv.at[j], fs.at[j - 1], fr.at[j - 1], (peer(j), s))
        for j in range(1, n_modes)
    ]

    for copy in r_copies:
        copy.wait_recv()
    for b in range(2 * REACH + 1):
        for z in range(4):
            field[z, 4 * b : 4 * b + 4, :] = r_recv[b, 4 * z : 4 * z + 4, :]
    mid = 4 * REACH
    start_r = [jnp.where(inside, field[z], 0.0) for z in range(4)]
    start_d = [r / theta for r in start_r]
    start_c = [d[mid : mid + 8] for d in start_d]

    def advance(k, carry):
        resid, direction, total = carry
        c_1, c_2 = cheb_c[k], cheb_c[CHEB + k]
        new_r, new_d, new_t = [], [], []
        for z in range(4):
            d = direction[z]
            applied = coup[6, z] * d
            applied = applied - coup[0, z] * pltpu.roll(d, 1, 0)
            applied = applied - coup[1, z] * pltpu.roll(d, padded - 1, 0)
            applied = applied - coup[2, z] * pltpu.roll(d, 1, 1)
            applied = applied - coup[3, z] * pltpu.roll(d, 127, 1)
            if z > 0:
                applied = applied - coup[4, z] * direction[z - 1]
            if z < 3:
                applied = applied - coup[5, z] * direction[z + 1]
            r = resid[z] - applied
            after = c_1 * d + c_2 * r
            new_r.append(r)
            new_d.append(after)
            new_t.append(total[z] + after[mid : mid + 8])
        return new_r, new_d, new_t

    _, _, correction = lax.fori_loop(0, CHEB - 1, advance, (start_r, start_d, start_c))
    for z in range(4):
        whole = half_ref[4 * z : 4 * z + 4, :] + correction[z][0:4]
        out_t[z] = pltpu.roll(whole, 96, 1)[:, 0:64]

    for copy in f_copies:
        copy.wait_recv()
    flux = ((f_recv[0] + f_recv[1]) + (f_recv[2] + f_recv[3])) / float(ORDINATES)
    for i in range(3):
        for z in range(4):
            at = 16 * i + 4 * z
            out_f[i, z] = flux[at : at + 4, 0:64] if at < 24 else flux[at - 24 : at - 20, 64:128]

    for copy in halo_copies + look_copies + window_copies + n_copies + f_copies + r_copies:
        copy.wait_send()


def solution(mesh):
    n_space, n_modes = mesh.shape["space"], mesh.shape["modes"]
    f32, i32 = jnp.float32, jnp.int32
    vmem = pl.BlockSpec(memory_space=pltpu.VMEM)
    dma = pltpu.SemaphoreType.DMA
    blocks = 2 * REACH + 1
    padded = 4 * blocks + 4

    def on_device(temp, source, label, lookup, vel, heat, rates, polar, azimuth):
        scratch = [
            pltpu.VMEM((4, 4, 256), f32), pltpu.VMEM((4, 4, 256), f32), pltpu.VMEM((4, 4, 256), i32),
            pltpu.VMEM((4, 1, 128), i32),
            pltpu.VMEM((80, 256), f32), pltpu.VMEM((80, 256), f32),
            pltpu.VMEM((11, 40, 128), f32), pltpu.VMEM((5, 24, 256), f32), pltpu.VMEM((2, 24 + 8, 128), f32),
            pltpu.VMEM((FT, 128, 8, 128), f32), pltpu.VMEM((48, 8, 128), i32),
            pltpu.VMEM((3 * FT, 8, 128), f32), pltpu.VMEM((FT, 8, 128), f32),
            pltpu.VMEM((16, 32, 8, 128), f32), pltpu.VMEM((16, 32, 8, 128), f32),
            pltpu.VMEM((4, 32, 8, 128), f32),
            pltpu.VMEM((256, 256), jnp.bfloat16),
            pltpu.VMEM((256, 128 * n_modes), jnp.bfloat16), pltpu.VMEM((256, 128 * n_modes), jnp.bfloat16),
            pltpu.VMEM((6, 1, 128), f32),
            pltpu.VMEM((16, 128), f32), pltpu.VMEM((16, 128), f32), pltpu.VMEM((blocks, 16, 128), f32),
            pltpu.VMEM((16, 256), f32), pltpu.VMEM((n_modes - 1, 16, 128), f32), pltpu.VMEM((n_modes, 16, 128), f32),
            pltpu.VMEM((48, 256), f32), pltpu.VMEM((n_modes - 1, 24, 128), f32), pltpu.VMEM((n_modes, 24, 128), f32),
            pltpu.VMEM((16, 128), f32), pltpu.VMEM((16, 128), f32), pltpu.VMEM((blocks, 16, 128), f32),
            pltpu.VMEM((4, padded, 128), f32), pltpu.VMEM((7, 4, padded, 128), f32),
            pltpu.VMEM((2 * CHEB, 1, 128), f32),
            dma((3,)), dma((3,)), dma((n_modes - 1,)), dma((n_modes - 1,)),
            dma((2 * REACH,)), dma((2 * REACH,)), dma((n_modes - 1,)), dma((n_modes - 1,)),
            dma((n_modes - 1,)), dma((n_modes - 1,)), dma((2 * REACH,)), dma((2 * REACH,)),
        ]
        call = pl.pallas_call(
            functools.partial(kernel, n_space, n_modes),
            out_shape=(
                pltpu.VMEM((4, 4, 64), f32),
                pltpu.VMEM((3, 4, 4, 64), f32),
            ),
            in_specs=[vmem] * 9 + [pl.BlockSpec(memory_space=pltpu.SMEM)],
            out_specs=(vmem, vmem),
            scratch_shapes=scratch,
            compiler_params=pltpu.CompilerParams(collective_id=0, has_side_effects=True),
        )
        return call(
            temp, source, label, lookup[None], vel[None], heat[None], rates.T,
            polar[None], azimuth[None], azimuth,
        )

    rows = P(None, "space", None)
    return jax.shard_map(
        on_device,
        mesh=mesh,
        in_specs=(rows, rows, rows, P("modes"), P(), P(), P(), P(), P()),
        out_specs=(P(None, "space", "modes"), P(None, None, "space", "modes")),
        check_vma=False,
    )
```

```python
import functools

import jax
import jax.numpy as jnp
from jax import lax
from jax.experimental import pallas as pl
from jax.experimental.pallas import tpu as pltpu
from jax.sharding import PartitionSpec as P

SPECTRAL_BINS = 40
ORDINATES = 60
CHEB = 16
FT = SPECTRAL_BINS // 8
REACH = 4
HALF_PI = 1.5707964
MESH = pl.DeviceIdType.MESH
OFFSETS = tuple(o for r in range(1, REACH + 1) for o in (r, -r))


def iota(shape, dim):
    return lax.broadcasted_iota(jnp.int32, shape, dim)


def permuted(x, chosen):
    rows = x.shape[0]
    first = x.astype(jnp.bfloat16)
    rest = x - first.astype(jnp.float32)
    second = rest.astype(jnp.bfloat16)
    third = (rest - second.astype(jnp.float32)).astype(jnp.bfloat16)
    stacked = jnp.concatenate([first, second, third], axis=0)
    out = jnp.dot(stacked, chosen, preferred_element_type=jnp.float32)
    return out[:rows] + (out[rows : 2 * rows] + out[2 * rows :])


def lookup(table, kind):
    return jnp.take_along_axis(
        table, kind, axis=1, mode="promise_in_bounds", wrap_negative_indices=False
    )


def ones_where(cond):
    return jnp.where(cond, 1.0, 0.0).astype(jnp.bfloat16)


def kernel(
    n_space, n_modes,
    t_ref, s_ref, l_ref, idx_ref, vel_ref, heat_ref, rates_ref, pol_ref, azi_ref, azs_ref,
    out_t, out_f,
    h_t, h_s, h_l, look, raw, il, dirs, wind, d_ref, cells, lab, inv_ref, p_sum, g_sum, q_of, cv, p_ref, g_ref, acc,
    w_int, w_num, w_flux, tables, t_win, l_send, l_recv, nq, n_send, n_recv, fq, f_send, f_recv,
    half_ref, r_send, r_recv, field, coup, cheb_c,
    tokens, hs, hr, ls, lr, ws, wr, ns, nr, fs, fr, rs, rr,
):
    m = lax.axis_index("modes")
    s = lax.axis_index("space")
    forward = m < n_modes // 2
    step = jnp.where(forward, 1, -1)

    def peer(j):
        return lax.rem(m + j, n_modes)

    def beside(o):
        return lax.rem(s + o + n_space, n_space)

    barrier = pltpu.get_barrier_semaphore()
    for j in range(1, n_modes):
        pl.semaphore_signal(barrier, inc=1, device_id=(peer(j), s), device_id_type=MESH)
    for o in (1, -1):
        pl.semaphore_signal(barrier, inc=1, device_id=(m, beside(o)), device_id_type=MESH)

    y0 = 64 * m - 32
    natural = ones_where(iota((256, 128), 0) == iota((256, 128), 1) + y0)
    for z in range(4):
        raw[pl.ds(4 * z, 4), :] = t_ref[z]
        raw[pl.ds(16 + 4 * z, 4), :] = l_ref[z].astype(jnp.float32)
    windows = permuted(raw[0:32, :], natural)
    t_win[...] = windows[0:16]
    l_send[...] = windows[16:32]
    l_recv[REACH] = windows[16:32]
    look[0] = jnp.zeros((1, 128), jnp.int32)
    look[0, :, 0:10] = idx_ref[...]

    spot = iota((32, 128), 0) == iota((32, 128), 1)

    def column(row_ref):
        row = jnp.concatenate([row_ref[...], jnp.zeros((1, 98), jnp.float32)], axis=1)
        picked = jnp.where(spot, jnp.broadcast_to(row, (32, 128)), 0.0)
        return jnp.broadcast_to(jnp.sum(picked, axis=1, keepdims=True), (32, 128))

    polar, azimuth = column(pol_ref), column(azi_ref)
    sign = jnp.where(forward, 1.0, -1.0)
    u_x = jnp.cos(polar)
    u_y = jnp.sin(polar) * jnp.cos(azimuth)
    u_z = jnp.sin(polar) * jnp.sin(azimuth)
    y_up = jnp.where(jnp.abs(azimuth) < HALF_PI, sign, -sign)
    z_up = jnp.where(azimuth > 0.0, sign, -sign)
    dirs[0, 0:32, :] = u_x
    dirs[1, 0:32, :] = jnp.abs(u_y)
    dirs[2, 0:32, :] = jnp.abs(u_z)
    dirs[3, 0:32, :] = u_x + jnp.abs(u_y) + jnp.abs(u_z)
    dirs[4, 0:32, :] = y_up
    dirs[5, 0:32, :] = z_up
    dirs[6, 0:32, :] = jnp.abs(u_y) / u_x
    dirs[7, 0:32, :] = jnp.abs(u_z) / u_x
    dirs[8, 0:32, :] = (u_x + jnp.abs(u_y) + jnp.abs(u_z)) / u_x
    dirs[9, 0:32, :] = sign * u_y / u_x
    dirs[10, 0:32, :] = sign * u_z / u_x

    y_of = 2 * (iota((256, 128), 0) & 127) + (iota((256, 128), 0) >> 7)
    lane = iota((256, 128), 1)
    for tile in range(2):
        w_int[:, tile * 128 : (tile + 1) * 128] = ones_where(iota((256, 128), 0) == 2 * lane + tile)
    for j in range(n_modes):
        w_num[:, j * 128 : (j + 1) * 128] = ones_where(y_of == lane + (64 * peer(j) - 32))
        w_flux[:, j * 128 : (j + 1) * 128] = ones_where((y_of == lane + 64 * peer(j)) & (lane < 64))

    pl.semaphore_wait(barrier, n_modes + 1)

    def described(source, target, send, recv, device):
        return pltpu.make_async_remote_copy(
            src_ref=source, dst_ref=target, send_sem=send, recv_sem=recv,
            device_id=device, device_id_type=MESH,
        )

    def remote(*of):
        copy = described(*of)
        copy.start()
        return copy

    def tell(level):
        for side in range(2):
            pl.semaphore_signal(
                tokens.at[side, level], inc=1, device_id=(m, beside(1 - 2 * side)), device_id_type=MESH
            )

    def hear(level):
        for side in range(2):
            pl.semaphore_wait(tokens.at[side, level], 1)

    down = (m, beside(step))
    halo_copies = [
        remote(t_ref, h_t, hs.at[0], hr.at[0], down),
        remote(s_ref, h_s, hs.at[1], hr.at[1], down),
        remote(l_ref, h_l, hs.at[2], hr.at[2], down),
    ]
    look_copies = [
        remote(look.at[0], look.at[j], ls.at[j - 1], lr.at[j - 1], (peer(j), s))
        for j in range(1, n_modes)
    ]
    tell(0)

    def window_copies():
        return [
            described(l_send, l_recv.at[REACH - o], ws.at[i], wr.at[i], (m, beside(o)))
            for i, o in enumerate(OFFSETS)
        ]

    for copy in look_copies:
        copy.wait_recv()
    freq = iota((SPECTRAL_BINS, 128), 0)
    slot = freq // 10
    spread = jnp.zeros((SPECTRAL_BINS, 128), jnp.float32)
    ordinal = jnp.zeros((SPECTRAL_BINS, 128), jnp.float32)
    for j in range(n_modes):
        row = jnp.broadcast_to(look[j].astype(jnp.float32), (SPECTRAL_BINS, 128))
        spread = jnp.where(slot == j, row, spread)
        owner = lax.rem(m + n_modes - j, n_modes)
        ordinal = jnp.where(slot == j, (10 * owner + 1).astype(jnp.float32), ordinal)
    within = freq - 10 * slot
    spectral = (ordinal + within.astype(jnp.float32)) / float(SPECTRAL_BINS)
    index = jnp.sum(
        jnp.where(iota((SPECTRAL_BINS, 128), 1) == within, spread, 0.0), axis=1, keepdims=True
    )
    chosen = iota((SPECTRAL_BINS, 64), 1).astype(jnp.float32) == index
    onehot = jnp.where(chosen, 1.0, 0.0)

    def looked_up(row):
        found = jnp.sum(onehot * row, axis=1, keepdims=True)
        return jnp.broadcast_to(found, (SPECTRAL_BINS, 128))

    velocity = looked_up(vel_ref[...])
    capacity = looked_up(heat_ref[...]) * spectral
    by_kind_of_f = [looked_up(rates_ref[k : k + 1, :]) for k in range(3)]
    kind_lane = lax.rem(iota((SPECTRAL_BINS, 128), 1), 3)
    rate = jnp.where(kind_lane == 0, by_kind_of_f[0], jnp.where(kind_lane == 1, by_kind_of_f[1], by_kind_of_f[2]))
    kinds = iota((1, 128), 1)
    rate_total = jnp.sum(capacity * rate, axis=0, keepdims=True)
    cond = capacity * velocity * velocity / (3.0 * rate)
    cond_total = jnp.sum(cond, axis=0, keepdims=True)
    conduct = cond_total / rate_total
    for k in range(3):
        def splat(row):
            one = jnp.sum(jnp.where(kinds == k, row, 0.0), axis=1, keepdims=True)
            return jnp.broadcast_to(one, (1, 128))
        tables[k] = splat(rate_total)
        tables[3 + k] = splat(conduct)
    cap_v = capacity * velocity
    inv_v = 1.0 / velocity
    for f in range(FT):
        for kind in range(3):
            q_of[3 * f + kind] = (by_kind_of_f[kind] / velocity)[8 * f : 8 * f + 8]
        cv[f] = cap_v[8 * f : 8 * f + 8]

    def row_of(ref, base, z):
        return jnp.where(forward, ref[z, base : base + 1, :], ref[z, 3 - base : 4 - base, :])

    def fill_cells(i):
        k, z = i // 4, i % 4
        for tile in range(2):
            cols = slice(tile * 128, (tile + 1) * 128)
            kind = jnp.broadcast_to(il[56 + i : 57 + i, cols], (8, 128)).astype(jnp.int32)
            is_0, is_1 = kind == 0, kind == 1
            temp = jnp.broadcast_to(il[4 + i : 5 + i, cols], (8, 128))
            heat = jnp.broadcast_to(il[32 + i : 33 + i, cols], (8, 128))
            spots = [(2 * a + b, 8 * k + 2 * abs(3 * a - z) + abs(b - tile)) for a in range(2) for b in range(2)]
            for order, at in spots:
                lab[order, at] = kind
            for f in range(FT):
                q = jnp.where(is_0, q_of[3 * f], jnp.where(is_1, q_of[3 * f + 1], q_of[3 * f + 2]))
                value = q * temp + inv_v[8 * f : 8 * f + 8] * heat
                for order, at in spots:
                    cells[order, f, at] = value
                if k >= 2:
                    value = cv[f] * value
                    for order, at in spots:
                        cells[order, f, 32 + at] = value

    for k in range(4):
        for z in range(4):
            at = 4 * k + z
            raw[at : at + 1, :] = row_of(t_ref, k, z)
            raw[16 + at : 17 + at, :] = row_of(s_ref, k, z)
            raw[32 + at : 33 + at, :] = row_of(l_ref, k, z).astype(jnp.float32)
    turned = permuted(raw[0:48, :], w_int[...])
    il[12:28, :] = turned[0:16]
    il[40:56, :] = turned[16:32]
    il[64:80, :] = turned[32:48]
    il[28:32, :] = jnp.zeros((4, 256), jnp.float32)
    for i in range(8, 24):
        fill_cells(i)

    for copy in halo_copies:
        copy.wait_recv()
    has = jnp.where(forward, s > 0, s < n_space - 1)
    raw[28:32, :] = jnp.zeros((4, 256), jnp.float32)
    for k in range(3):
        for z in range(4):
            at = 4 * k + z
            raw[at : at + 1, :] = jnp.where(has, row_of(h_t, k + 1, z), 0.0)
            if k > 0:
                raw[8 + at : 9 + at, :] = jnp.where(has, row_of(h_s, k + 1, z), 0.0)
                raw[16 + at : 17 + at, :] = row_of(h_l, k + 1, z).astype(jnp.float32)
    turned = permuted(raw[0:32, :], w_int[...])
    il[0:12, :] = turned[0:12]
    il[32:40, :] = turned[12:20]
    il[56:64, :] = turned[20:28]
    for i in range(8):
        fill_cells(i)

    for k in range(7):
        for z in range(4):
            at = 4 * k + z
            raw[at : at + 1, :] = il[4 * k + 3 - z : 4 * k + 4 - z, :]
    level = iota((24, 128), 0) & 3
    tile_lane = iota((24, 128), 1)
    for a, rows in enumerate((il, raw)):
        for b in range(2):
            near = [slice(0, 128), slice(128, 256)] if b == 0 else [slice(128, 256), slice(0, 128)]
            for q in range(2):
                wind[2 * a + b, 0, q] = rows[0:24, near[q]]
                wind[2 * a + b, 2, q] = jnp.where(level == 0, 0.0, rows[3:27, near[q]])
            edge, turn = (0, 1) if b == 0 else (127, 127)
            wind[2 * a + b, 1, 0] = jnp.where(tile_lane == edge, 0.0, pltpu.roll(rows[4:28, near[1]], turn, 1))
            wind[2 * a + b, 1, 1] = rows[4:28, near[0]]

    lanes8 = iota((8, 128), 1)
    first = lax.rem(m, n_modes // 2) * 15

    def upwind_order(j):
        angle = azs_ref[first + j]
        ahead = jnp.logical_xor(jnp.abs(angle) < HALF_PI, jnp.logical_not(forward))
        up = jnp.logical_xor(angle > 0.0, jnp.logical_not(forward))
        return up, ahead

    both = range(2)
    cell = [(z, q) for z in range(4) for q in both]

    def stored_at(j):
        up, ahead = upwind_order(j)
        levels = [jnp.where(up, z, 3 - z) for z in range(4)]
        tiles = [jnp.where(ahead, q, 1 - q) for q in both]
        return [[2 * levels[z] + tiles[t] for t in both] for z in range(4)]

    def numerator(j):
        place = stored_at(jnp.maximum(j, 0))
        held = jnp.where(j < 0, 15, j)
        for k in range(4):
            for z, t in cell:
                acc[0, 8 * k + 2 * z + t] += p_ref[held, 8 * k + place[z][t]]

    for i in range(32):
        acc[0, i] = jnp.zeros((8, 128), jnp.float32)
        p_ref[15, i] = jnp.zeros((8, 128), jnp.float32)
    hear(0)
    tell(1)

    def per_direction(j, _):
        @pl.when(j == 3)
        def _():
            hear(1)
            tell(2)

        @pl.when(j == 6)
        def _():
            hear(2)
            for copy in window_copies():
                copy.start()

        numerator(j - 1)

        def coef(which):
            return dirs[which, pl.ds(first + j, 8, stride=0), :]

        def tall(row):
            return jnp.concatenate([row] * 3, axis=0)

        up, ahead = upwind_order(j)
        order = jnp.where(up, 0, 2) + jnp.where(ahead, 0, 1)
        turn = jnp.where(ahead, 1, 127)
        a_x, a_y, a_z, a_sum = tall(coef(0)), tall(coef(1)), tall(coef(2)), coef(3)
        for q in both:
            d_ref[q, 0:24, :] = a_x * wind[order, 0, q] + (a_y * wind[order, 1, q] + a_z * wind[order, 2, q])
        r_y, r_z, ratio = coef(6), coef(7), coef(8)
        r_edge = jnp.where(lanes8 == jnp.where(ahead, 0, 127), 0.0, r_y)
        slope = coef(0)
        weights = [[slope / (a_sum + q_of[3 * f + kind]) for kind in range(3)] for f in range(FT)]
        for at in range(48):
            kind = lab[order, at]
            is_0, is_1 = kind == 0, kind == 1
            for f in range(FT):
                w = weights[f]
                inv_ref[f, at] = jnp.where(is_0, w[0], jnp.where(is_1, w[1], w[2]))
        for i in range(32):
            p_sum[i] = jnp.zeros((8, 128), jnp.float32)
            g_sum[i] = jnp.zeros((8, 128), jnp.float32)

        def block(f, last):
            scaled = (cv[f], cv[f] * r_y, cv[f] * r_edge, cv[f] * r_z)
            h1_before = h2_before = None

            def gathered(before, now, scale, source):
                c_x, c_y, c_edge, c_z = scale
                out = {}
                for z in range(4):
                    along = (c_edge * pltpu.roll(now[z, 1], turn, 1), c_y * now[z, 0])
                    for q in both:
                        behind = before[z, q] if c_x is None else c_x * before[z, q]
                        total = (behind + along[q]) + source(2 * z + q)
                        out[z, q] = total + c_z * now[z - 1, q] if z > 0 else total
                return out

            for k in range(6):
                inv = {(z, q): inv_ref[f, 8 * k + 2 * z + q] for z, q in cell}
                here = {(z, q): cells[order, f, 8 * k + 2 * z + q] for z, q in cell}
                h1 = {
                    (z, q): inv[z, q] * (d_ref[q, pl.ds(4 * k + z, 8, stride=0), :] + here[z, q])
                    for z, q in cell
                }
                h2 = None
                if k >= 1:
                    total = gathered(h1_before, h1, (None, r_y, r_edge, r_z), lambda i: here[i // 2, i % 2])
                    h2 = {c: inv[c] * total[c] for c in cell}
                if k >= 2:
                    total = gathered(h2_before, h2, scaled, lambda i: cells[order, f, 32 + 8 * k + i])
                    for z, q in cell:
                        i = 8 * (k - 2) + 2 * z + q
                        p_new = p_sum[i] + total[z, q]
                        g_new = g_sum[i] + inv[z, q] * total[z, q]
                        if last:
                            p_ref[j, i] = p_new - ratio * g_new
                            g_ref[j, i] = g_new
                        else:
                            p_sum[i] = p_new
                            g_sum[i] = g_new
                h1_before, h2_before = h1, h2

        def per_block(f, _):
            block(f, False)
            return 0

        lax.fori_loop(0, FT - 1, per_block, 0)
        block(FT - 1, True)
        return 0

    lax.fori_loop(0, 15, per_direction, 0)

    numerator(14)
    zero = jnp.zeros((8, 128), jnp.float32)

    def fluxes():
        for k in range(4):
            def flux_of(j, totals):
                v_y = dirs[9, pl.ds(first + j, 8, stride=0), :]
                v_z = dirs[10, pl.ds(first + j, 8, stride=0), :]
                place = stored_at(j)
                out = []
                for z, t in cell:
                    flow = g_ref[j, 8 * k + place[z][t]]
                    n = len(out)
                    out += [totals[n] + flow, totals[n + 1] + v_y * flow, totals[n + 2] + v_z * flow]
                return out

            found = lax.fori_loop(0, 15, flux_of, [zero] * 24)
            for n in range(8):
                acc[1, 8 * k + n] = sign * found[3 * n]
                acc[2, 8 * k + n] = found[3 * n + 1]
                acc[3, 8 * k + n] = found[3 * n + 2]

    def summed(which, target, base):
        for z in range(4):
            for t in range(2):
                found = [jnp.sum(acc[which, 8 * k + 2 * z + t], axis=0, keepdims=True) for k in range(4)]
                for x in range(4):
                    at = base + 4 * z + x
                    row = jnp.where(forward, found[x], found[3 - x])
                    target[at : at + 1, t * 128 : (t + 1) * 128] = row

    summed(0, nq, 0)
    moved = permuted(nq[...], w_num[...])
    n_recv[0] = moved[:, 0:128]
    for j in range(1, n_modes):
        n_send[j - 1] = moved[:, j * 128 : (j + 1) * 128]
    n_copies = [
        remote(n_send.at[j - 1], n_recv.at[j], ns.at[j - 1], nr.at[j - 1], (peer(j), s))
        for j in range(1, n_modes)
    ]
    for copy in window_copies():
        copy.wait_recv()
    for b in range(2 * REACH + 1):
        for z in range(4):
            field[z, 4 * b : 4 * b + 4, :] = l_recv[b, 4 * z : 4 * z + 4, :]
    rows = 4 * (2 * REACH + 1)
    padded = rows + 4
    for z in range(4):
        field[z, rows:padded, :] = jnp.zeros((4, 128), jnp.float32)
    x_of = iota((padded, 128), 0) + 4 * (s - REACH)
    y_of_lane = iota((padded, 128), 1) + y0
    inside = (
        (x_of >= 0) & (x_of < 4 * n_space) & (iota((padded, 128), 0) < rows)
        & (y_of_lane >= 0) & (y_of_lane < 256)
    )

    def by_kind(label, base):
        return jnp.where(label == 0.0, tables[base], jnp.where(label == 1.0, tables[base + 1], tables[base + 2]))

    kappa = [jnp.where(inside, by_kind(field[z], 3), 0.0) for z in range(4)]

    def link(here, there):
        mean = 0.5 * (here + there)
        return jnp.where(here > 0.0, mean, 0.0), jnp.where((here > 0.0) & (there > 0.0), mean, 0.0)

    for z in range(4):
        here = kappa[z]
        none = jnp.zeros_like(here)
        around = [
            pltpu.roll(here, 1, 0), pltpu.roll(here, padded - 1, 0),
            pltpu.roll(here, 1, 1), pltpu.roll(here, 127, 1),
            kappa[z - 1] if z > 0 else none, kappa[z + 1] if z < 3 else none,
        ]
        diagonal = jnp.full_like(here, 1.0)
        for which, there in enumerate(around):
            whole, joint = link(here, there)
            diagonal = diagonal + whole
            coup[which, z] = joint
        coup[6, z] = diagonal

    top = 1.0 + 12.0 * jnp.maximum(jnp.maximum(tables[3], tables[4]), tables[5])
    theta = (top + 1.0) / 2.0
    delta = (top - 1.0) / 2.0
    sigma = theta / delta
    rho = 1.0 / sigma
    for k in range(CHEB - 1):
        rho_new = 1.0 / (2.0 * sigma - rho)
        cheb_c[k] = rho_new * rho
        cheb_c[CHEB + k] = 2.0 * rho_new / delta
        rho = rho_new

    for copy in n_copies:
        copy.wait_recv()
    numer = (n_recv[0] + n_recv[1]) + (n_recv[2] + n_recv[3])
    here = l_recv[REACH]
    half = numer / (float(ORDINATES) * by_kind(here, 0))
    mismatch = half - t_win[...]
    half_ref[...] = half
    r_send[...] = mismatch
    r_recv[REACH] = mismatch
    r_copies = [
        remote(r_send, r_recv.at[REACH - o], rs.at[i], rr.at[i], (m, beside(o)))
        for i, o in reversed(tuple(enumerate(OFFSETS)))
    ]

    fluxes()
    for i in range(3):
        summed(1 + i, fq, 16 * i)
    moved = permuted(fq[...], w_flux[...])
    for j in range(n_modes):
        part = moved[:, j * 128 : (j + 1) * 128]
        packed = part[0:24] + pltpu.roll(part[24:48], 64, 1)
        if j == 0:
            f_recv[0] = packed
        else:
            f_send[j - 1] = packed
    f_copies = [
        remote(f_send.at[j - 1], f_recv.at[j], fs.at[j - 1], fr.at[j - 1], (peer(j), s))
        for j in range(1, n_modes)
    ]

    for copy in r_copies:
        copy.wait_recv()
    for b in range(2 * REACH + 1):
        for z in range(4):
            field[z, 4 * b : 4 * b + 4, :] = r_recv[b, 4 * z : 4 * z + 4, :]
    mid = 4 * REACH
    start_r = [jnp.where(inside, field[z], 0.0) for z in range(4)]
    start_d = [r / theta for r in start_r]
    start_c = [d[mid : mid + 8] for d in start_d]

    def advance(k, carry):
        resid, direction, total = carry
        c_1, c_2 = cheb_c[k], cheb_c[CHEB + k]
        new_r, new_d, new_t = [], [], []
        for z in range(4):
            d = direction[z]
            applied = coup[6, z] * d
            applied = applied - coup[0, z] * pltpu.roll(d, 1, 0)
            applied = applied - coup[1, z] * pltpu.roll(d, padded - 1, 0)
            applied = applied - coup[2, z] * pltpu.roll(d, 1, 1)
            applied = applied - coup[3, z] * pltpu.roll(d, 127, 1)
            if z > 0:
                applied = applied - coup[4, z] * direction[z - 1]
            if z < 3:
                applied = applied - coup[5, z] * direction[z + 1]
            r = resid[z] - applied
            after = c_1 * d + c_2 * r
            new_r.append(r)
            new_d.append(after)
            new_t.append(total[z] + after[mid : mid + 8])
        return new_r, new_d, new_t

    _, _, correction = lax.fori_loop(0, CHEB - 1, advance, (start_r, start_d, start_c))
    for z in range(4):
        whole = half_ref[4 * z : 4 * z + 4, :] + correction[z][0:4]
        out_t[z] = pltpu.roll(whole, 96, 1)[:, 0:64]

    for copy in f_copies:
        copy.wait_recv()
    flux = ((f_recv[0] + f_recv[1]) + (f_recv[2] + f_recv[3])) / float(ORDINATES)
    for i in range(3):
        for z in range(4):
            at = 16 * i + 4 * z
            out_f[i, z] = flux[at : at + 4, 0:64] if at < 24 else flux[at - 24 : at - 20, 64:128]

    for copy in halo_copies + look_copies + window_copies() + n_copies + f_copies + r_copies:
        copy.wait_send()


def solution(mesh):
    n_space, n_modes = mesh.shape["space"], mesh.shape["modes"]
    f32, i32 = jnp.float32, jnp.int32
    vmem = pl.BlockSpec(memory_space=pltpu.VMEM)
    dma = pltpu.SemaphoreType.DMA
    blocks = 2 * REACH + 1
    padded = 4 * blocks + 4

    def on_device(temp, source, label, lookup, vel, heat, rates, polar, azimuth):
        scratch = [
            pltpu.VMEM((4, 4, 256), f32), pltpu.VMEM((4, 4, 256), f32), pltpu.VMEM((4, 4, 256), i32),
            pltpu.VMEM((4, 1, 128), i32),
            pltpu.VMEM((80, 256), f32), pltpu.VMEM((80, 256), f32),
            pltpu.VMEM((11, 40, 128), f32), pltpu.VMEM((4, 3, 2, 24, 128), f32), pltpu.VMEM((2, 24 + 8, 128), f32),
            pltpu.VMEM((4, FT, 80, 8, 128), f32), pltpu.VMEM((4, 48, 8, 128), i32),
            pltpu.VMEM((FT, 48, 8, 128), f32), pltpu.VMEM((32, 8, 128), f32), pltpu.VMEM((32, 8, 128), f32),
            pltpu.VMEM((3 * FT, 8, 128), f32), pltpu.VMEM((FT, 8, 128), f32),
            pltpu.VMEM((16, 32, 8, 128), f32), pltpu.VMEM((15, 32, 8, 128), f32),
            pltpu.VMEM((4, 32, 8, 128), f32),
            pltpu.VMEM((256, 256), jnp.bfloat16),
            pltpu.VMEM((256, 128 * n_modes), jnp.bfloat16), pltpu.VMEM((256, 128 * n_modes), jnp.bfloat16),
            pltpu.VMEM((6, 1, 128), f32),
            pltpu.VMEM((16, 128), f32), pltpu.VMEM((16, 128), f32), pltpu.VMEM((blocks, 16, 128), f32),
            pltpu.VMEM((16, 256), f32), pltpu.VMEM((n_modes - 1, 16, 128), f32), pltpu.VMEM((n_modes, 16, 128), f32),
            pltpu.VMEM((48, 256), f32), pltpu.VMEM((n_modes - 1, 24, 128), f32), pltpu.VMEM((n_modes, 24, 128), f32),
            pltpu.VMEM((16, 128), f32), pltpu.VMEM((16, 128), f32), pltpu.VMEM((blocks, 16, 128), f32),
            pltpu.VMEM((4, padded, 128), f32), pltpu.VMEM((7, 4, padded, 128), f32),
            pltpu.VMEM((2 * CHEB, 1, 128), f32),
            pltpu.SemaphoreType.REGULAR((2, 3)),
            dma((3,)), dma((3,)), dma((n_modes - 1,)), dma((n_modes - 1,)),
            dma((2 * REACH,)), dma((2 * REACH,)), dma((n_modes - 1,)), dma((n_modes - 1,)),
            dma((n_modes - 1,)), dma((n_modes - 1,)), dma((2 * REACH,)), dma((2 * REACH,)),
        ]
        call = pl.pallas_call(
            functools.partial(kernel, n_space, n_modes),
            out_shape=(
                pltpu.VMEM((4, 4, 64), f32),
                pltpu.VMEM((3, 4, 4, 64), f32),
            ),
            in_specs=[vmem] * 9 + [pl.BlockSpec(memory_space=pltpu.SMEM)],
            out_specs=(vmem, vmem),
            scratch_shapes=scratch,
            compiler_params=pltpu.CompilerParams(collective_id=0, has_side_effects=True),
        )
        return call(
            temp, source, label, lookup[None], vel[None], heat[None], rates.T,
            polar[None], azimuth[None], azimuth,
        )

    rows = P(None, "space", None)
    return jax.shard_map(
        on_device,
        mesh=mesh,
        in_specs=(rows, rows, rows, P("modes"), P(), P(), P(), P(), P()),
        out_specs=(P(None, "space", "modes"), P(None, None, "space", "modes")),
        check_vma=False,
    )
```

```python
import functools

import jax
import jax.numpy as jnp
from jax import lax
from jax.experimental import pallas as pl
from jax.experimental.pallas import tpu as pltpu
from jax.sharding import PartitionSpec as P

SPECTRAL_BINS = 40
ORDINATES = 60
CHEB = 16
FT = SPECTRAL_BINS // 8
REACH = 4
HALF_PI = 1.5707964
MESH = pl.DeviceIdType.MESH
OFFSETS = tuple(o for r in range(1, REACH + 1) for o in (r, -r))


def iota(shape, dim):
    return lax.broadcasted_iota(jnp.int32, shape, dim)


def permuted(x, chosen):
    rows = x.shape[0]
    first = x.astype(jnp.bfloat16)
    rest = x - first.astype(jnp.float32)
    second = rest.astype(jnp.bfloat16)
    third = (rest - second.astype(jnp.float32)).astype(jnp.bfloat16)
    stacked = jnp.concatenate([first, second, third], axis=0)
    out = jnp.dot(stacked, chosen, preferred_element_type=jnp.float32)
    return out[:rows] + (out[rows : 2 * rows] + out[2 * rows :])


def lookup(table, kind):
    return jnp.take_along_axis(
        table, kind, axis=1, mode="promise_in_bounds", wrap_negative_indices=False
    )


def ones_where(cond):
    return jnp.where(cond, 1.0, 0.0).astype(jnp.bfloat16)


def kernel(
    n_space, n_modes,
    t_ref, s_ref, l_ref, idx_ref, vel_ref, heat_ref, rates_ref, pol_ref, azi_ref, azs_ref,
    out_t, out_f,
    h_t, h_s, h_l, look, raw, il, dirs, wind, d_ref, cells, lab, inv_ref, p_sum, g_sum, q_of, cv, p_ref, g_ref, acc,
    w_int, w_num, w_flux, tables, t_win, l_send, l_recv, nq, n_send, n_recv, fq, f_send, f_recv,
    half_ref, r_send, r_recv, field, coup, cheb_c,
    tokens, hs, hr, ls, lr, ws, wr, ns, nr, fs, fr, rs, rr,
):
    m = lax.axis_index("modes")
    s = lax.axis_index("space")
    forward = m < n_modes // 2
    step = jnp.where(forward, 1, -1)

    def peer(j):
        return lax.rem(m + j, n_modes)

    def beside(o):
        return lax.rem(s + o + n_space, n_space)

    barrier = pltpu.get_barrier_semaphore()
    for j in range(1, n_modes):
        pl.semaphore_signal(barrier, inc=1, device_id=(peer(j), s), device_id_type=MESH)
    for o in (1, -1):
        pl.semaphore_signal(barrier, inc=1, device_id=(m, beside(o)), device_id_type=MESH)

    y0 = 64 * m - 32
    natural = ones_where(iota((256, 128), 0) == iota((256, 128), 1) + y0)
    for z in range(4):
        raw[pl.ds(4 * z, 4), :] = t_ref[z]
        raw[pl.ds(16 + 4 * z, 4), :] = l_ref[z].astype(jnp.float32)
    windows = permuted(raw[0:32, :], natural)
    t_win[...] = windows[0:16]
    l_send[...] = windows[16:32]
    l_recv[REACH] = windows[16:32]
    look[0] = jnp.zeros((1, 128), jnp.int32)
    look[0, :, 0:10] = idx_ref[...]

    spot = iota((32, 128), 0) == iota((32, 128), 1)

    def column(row_ref):
        row = jnp.concatenate([row_ref[...], jnp.zeros((1, 98), jnp.float32)], axis=1)
        picked = jnp.where(spot, jnp.broadcast_to(row, (32, 128)), 0.0)
        return jnp.broadcast_to(jnp.sum(picked, axis=1, keepdims=True), (32, 128))

    polar, azimuth = column(pol_ref), column(azi_ref)
    sign = jnp.where(forward, 1.0, -1.0)
    u_x = jnp.cos(polar)
    u_y = jnp.sin(polar) * jnp.cos(azimuth)
    u_z = jnp.sin(polar) * jnp.sin(azimuth)
    y_up = jnp.where(jnp.abs(azimuth) < HALF_PI, sign, -sign)
    z_up = jnp.where(azimuth > 0.0, sign, -sign)
    dirs[0, 0:32, :] = u_x
    dirs[1, 0:32, :] = jnp.abs(u_y)
    dirs[2, 0:32, :] = jnp.abs(u_z)
    dirs[3, 0:32, :] = u_x + jnp.abs(u_y) + jnp.abs(u_z)
    dirs[4, 0:32, :] = y_up
    dirs[5, 0:32, :] = z_up
    dirs[6, 0:32, :] = jnp.abs(u_y) / u_x
    dirs[7, 0:32, :] = jnp.abs(u_z) / u_x
    dirs[8, 0:32, :] = (u_x + jnp.abs(u_y) + jnp.abs(u_z)) / u_x
    dirs[9, 0:32, :] = sign * u_y / u_x
    dirs[10, 0:32, :] = sign * u_z / u_x

    y_of = 2 * (iota((256, 128), 0) & 127) + (iota((256, 128), 0) >> 7)
    lane = iota((256, 128), 1)
    for tile in range(2):
        w_int[:, tile * 128 : (tile + 1) * 128] = ones_where(iota((256, 128), 0) == 2 * lane + tile)
    for j in range(n_modes):
        w_num[:, j * 128 : (j + 1) * 128] = ones_where(y_of == lane + (64 * peer(j) - 32))
        w_flux[:, j * 128 : (j + 1) * 128] = ones_where((y_of == lane + 64 * peer(j)) & (lane < 64))

    pl.semaphore_wait(barrier, n_modes + 1)

    def described(source, target, send, recv, device):
        return pltpu.make_async_remote_copy(
            src_ref=source, dst_ref=target, send_sem=send, recv_sem=recv,
            device_id=device, device_id_type=MESH,
        )

    def remote(*of):
        copy = described(*of)
        copy.start()
        return copy

    def tell(level):
        for side in range(2):
            pl.semaphore_signal(
                tokens.at[side, level], inc=1, device_id=(m, beside(1 - 2 * side)), device_id_type=MESH
            )

    def hear(level):
        for side in range(2):
            pl.semaphore_wait(tokens.at[side, level], 1)

    down = (m, beside(step))
    halo_copies = [
        remote(t_ref, h_t, hs.at[0], hr.at[0], down),
        remote(s_ref, h_s, hs.at[1], hr.at[1], down),
        remote(l_ref, h_l, hs.at[2], hr.at[2], down),
    ]
    look_copies = [
        remote(look.at[0], look.at[j], ls.at[j - 1], lr.at[j - 1], (peer(j), s))
        for j in range(1, n_modes)
    ]
    tell(0)

    def window_copies():
        return [
            described(l_send, l_recv.at[REACH - o], ws.at[i], wr.at[i], (m, beside(o)))
            for i, o in enumerate(OFFSETS)
        ]

    for copy in look_copies:
        copy.wait_recv()
    freq = iota((SPECTRAL_BINS, 128), 0)
    slot = freq // 10
    spread = jnp.zeros((SPECTRAL_BINS, 128), jnp.float32)
    ordinal = jnp.zeros((SPECTRAL_BINS, 128), jnp.float32)
    for j in range(n_modes):
        row = jnp.broadcast_to(look[j].astype(jnp.float32), (SPECTRAL_BINS, 128))
        spread = jnp.where(slot == j, row, spread)
        owner = lax.rem(m + n_modes - j, n_modes)
        ordinal = jnp.where(slot == j, (10 * owner + 1).astype(jnp.float32), ordinal)
    within = freq - 10 * slot
    spectral = (ordinal + within.astype(jnp.float32)) / float(SPECTRAL_BINS)
    index = jnp.sum(
        jnp.where(iota((SPECTRAL_BINS, 128), 1) == within, spread, 0.0), axis=1, keepdims=True
    )
    chosen = iota((SPECTRAL_BINS, 64), 1).astype(jnp.float32) == index
    onehot = jnp.where(chosen, 1.0, 0.0)

    def looked_up(row):
        found = jnp.sum(onehot * row, axis=1, keepdims=True)
        return jnp.broadcast_to(found, (SPECTRAL_BINS, 128))

    velocity = looked_up(vel_ref[...])
    capacity = looked_up(heat_ref[...]) * spectral
    by_kind_of_f = [looked_up(rates_ref[k : k + 1, :]) for k in range(3)]
    kind_lane = lax.rem(iota((SPECTRAL_BINS, 128), 1), 3)
    rate = jnp.where(kind_lane == 0, by_kind_of_f[0], jnp.where(kind_lane == 1, by_kind_of_f[1], by_kind_of_f[2]))
    kinds = iota((1, 128), 1)
    rate_total = jnp.sum(capacity * rate, axis=0, keepdims=True)
    cond = capacity * velocity * velocity / (3.0 * rate)
    cond_total = jnp.sum(cond, axis=0, keepdims=True)
    conduct = cond_total / rate_total
    for k in range(3):
        def splat(row):
            one = jnp.sum(jnp.where(kinds == k, row, 0.0), axis=1, keepdims=True)
            return jnp.broadcast_to(one, (1, 128))
        tables[k] = splat(rate_total)
        tables[3 + k] = splat(conduct)
    cap_v = capacity * velocity
    inv_v = 1.0 / velocity
    for f in range(FT):
        for kind in range(3):
            q_of[3 * f + kind] = (by_kind_of_f[kind] / velocity)[8 * f : 8 * f + 8]
        cv[f] = cap_v[8 * f : 8 * f + 8]

    def row_of(ref, base, z):
        return jnp.where(forward, ref[z, base : base + 1, :], ref[z, 3 - base : 4 - base, :])

    def fill_cells(i):
        k, z = i // 4, i % 4
        for tile in range(2):
            cols = slice(tile * 128, (tile + 1) * 128)
            kind = jnp.broadcast_to(il[56 + i : 57 + i, cols], (8, 128)).astype(jnp.int32)
            is_0, is_1 = kind == 0, kind == 1
            temp = jnp.broadcast_to(il[4 + i : 5 + i, cols], (8, 128))
            heat = jnp.broadcast_to(il[32 + i : 33 + i, cols], (8, 128))
            spots = [(2 * a + b, 8 * k + 2 * abs(3 * a - z) + abs(b - tile)) for a in range(2) for b in range(2)]
            for order, at in spots:
                lab[order, at] = kind
            for f in range(FT):
                q = jnp.where(is_0, q_of[3 * f], jnp.where(is_1, q_of[3 * f + 1], q_of[3 * f + 2]))
                value = q * temp + inv_v[8 * f : 8 * f + 8] * heat
                for order, at in spots:
                    cells[order, f, at] = value
                if k >= 2:
                    value = cv[f] * value
                    for order, at in spots:
                        cells[order, f, 32 + at] = value

    for k in range(4):
        for z in range(4):
            at = 4 * k + z
            raw[at : at + 1, :] = row_of(t_ref, k, z)
            raw[16 + at : 17 + at, :] = row_of(s_ref, k, z)
            raw[32 + at : 33 + at, :] = row_of(l_ref, k, z).astype(jnp.float32)
    turned = permuted(raw[0:48, :], w_int[...])
    il[12:28, :] = turned[0:16]
    il[40:56, :] = turned[16:32]
    il[64:80, :] = turned[32:48]
    il[28:32, :] = jnp.zeros((4, 256), jnp.float32)
    for i in range(8, 24):
        fill_cells(i)

    for copy in halo_copies:
        copy.wait_recv()
    has = jnp.where(forward, s > 0, s < n_space - 1)
    raw[28:32, :] = jnp.zeros((4, 256), jnp.float32)
    for k in range(3):
        for z in range(4):
            at = 4 * k + z
            raw[at : at + 1, :] = jnp.where(has, row_of(h_t, k + 1, z), 0.0)
            if k > 0:
                raw[8 + at : 9 + at, :] = jnp.where(has, row_of(h_s, k + 1, z), 0.0)
                raw[16 + at : 17 + at, :] = row_of(h_l, k + 1, z).astype(jnp.float32)
    turned = permuted(raw[0:32, :], w_int[...])
    il[0:12, :] = turned[0:12]
    il[32:40, :] = turned[12:20]
    il[56:64, :] = turned[20:28]
    for i in range(8):
        fill_cells(i)

    for k in range(7):
        for z in range(4):
            at = 4 * k + z
            raw[at : at + 1, :] = il[4 * k + 3 - z : 4 * k + 4 - z, :]
    level = iota((24, 128), 0) & 3
    tile_lane = iota((24, 128), 1)
    for a, rows in enumerate((il, raw)):
        for b in range(2):
            near = [slice(0, 128), slice(128, 256)] if b == 0 else [slice(128, 256), slice(0, 128)]
            for q in range(2):
                wind[2 * a + b, 0, q] = rows[0:24, near[q]]
                wind[2 * a + b, 2, q] = jnp.where(level == 0, 0.0, rows[3:27, near[q]])
            edge, turn = (0, 1) if b == 0 else (127, 127)
            wind[2 * a + b, 1, 0] = jnp.where(tile_lane == edge, 0.0, pltpu.roll(rows[4:28, near[1]], turn, 1))
            wind[2 * a + b, 1, 1] = rows[4:28, near[0]]

    lanes8 = iota((8, 128), 1)
    first = lax.rem(m, n_modes // 2) * 15

    def upwind_order(j):
        angle = azs_ref[first + j]
        ahead = jnp.logical_xor(jnp.abs(angle) < HALF_PI, jnp.logical_not(forward))
        up = jnp.logical_xor(angle > 0.0, jnp.logical_not(forward))
        return up, ahead

    both = range(2)
    cell = [(z, q) for z in range(4) for q in both]

    def stored_at(j):
        up, ahead = upwind_order(j)
        levels = [jnp.where(up, z, 3 - z) for z in range(4)]
        tiles = [jnp.where(ahead, q, 1 - q) for q in both]
        return [[2 * levels[z] + tiles[t] for t in both] for z in range(4)]

    def numerator(j):
        place = stored_at(jnp.maximum(j, 0))
        held = jnp.where(j < 0, 15, j)
        for k in range(4):
            for z, t in cell:
                acc[0, 8 * k + 2 * z + t] += p_ref[held, 8 * k + place[z][t]]

    for i in range(32):
        acc[0, i] = jnp.zeros((8, 128), jnp.float32)
        p_ref[15, i] = jnp.zeros((8, 128), jnp.float32)
    hear(0)
    tell(1)

    def per_direction(j, _):
        @pl.when(j == 3)
        def _():
            hear(1)
            tell(2)

        @pl.when(j == 6)
        def _():
            hear(2)
            for copy in window_copies():
                copy.start()

        numerator(j - 1)

        def coef(which):
            return dirs[which, pl.ds(first + j, 8, stride=0), :]

        def tall(row):
            return jnp.concatenate([row] * 3, axis=0)

        up, ahead = upwind_order(j)
        order = jnp.where(up, 0, 2) + jnp.where(ahead, 0, 1)
        turn = jnp.where(ahead, 1, 127)
        a_x, a_y, a_z, a_sum = tall(coef(0)), tall(coef(1)), tall(coef(2)), coef(3)
        for q in both:
            d_ref[q, 0:24, :] = a_x * wind[order, 0, q] + (a_y * wind[order, 1, q] + a_z * wind[order, 2, q])
        r_y, r_z, ratio = coef(6), coef(7), coef(8)
        r_edge = jnp.where(lanes8 == jnp.where(ahead, 0, 127), 0.0, r_y)
        slope = coef(0)
        weights = [[slope / (a_sum + q_of[3 * f + kind]) for kind in range(3)] for f in range(FT)]
        for at in range(48):
            kind = lab[order, at]
            is_0, is_1 = kind == 0, kind == 1
            for f in range(FT):
                w = weights[f]
                inv_ref[f, at] = jnp.where(is_0, w[0], jnp.where(is_1, w[1], w[2]))
        for i in range(32):
            p_sum[i] = jnp.zeros((8, 128), jnp.float32)
            g_sum[i] = jnp.zeros((8, 128), jnp.float32)

        def block(f, last):
            scaled = (cv[f], cv[f] * r_y, cv[f] * r_edge, cv[f] * r_z)
            h1_before = h2_before = None

            def gathered(before, now, scale, source):
                c_x, c_y, c_edge, c_z = scale
                out = {}
                for z in range(4):
                    along = (c_edge * pltpu.roll(now[z, 1], turn, 1), c_y * now[z, 0])
                    for q in both:
                        behind = before[z, q] if c_x is None else c_x * before[z, q]
                        total = (behind + along[q]) + source(2 * z + q)
                        out[z, q] = total + c_z * now[z - 1, q] if z > 0 else total
                return out

            for k in range(6):
                inv = {(z, q): inv_ref[f, 8 * k + 2 * z + q] for z, q in cell}
                here = {(z, q): cells[order, f, 8 * k + 2 * z + q] for z, q in cell}
                h1 = {
                    (z, q): inv[z, q] * (d_ref[q, pl.ds(4 * k + z, 8, stride=0), :] + here[z, q])
                    for z, q in cell
                }
                h2 = None
                if k >= 1:
                    total = gathered(h1_before, h1, (None, r_y, r_edge, r_z), lambda i: here[i // 2, i % 2])
                    h2 = {c: inv[c] * total[c] for c in cell}
                if k >= 2:
                    total = gathered(h2_before, h2, scaled, lambda i: cells[order, f, 32 + 8 * k + i])
                    for z, q in cell:
                        i = 8 * (k - 2) + 2 * z + q
                        p_new = p_sum[i] + total[z, q]
                        g_new = g_sum[i] + inv[z, q] * total[z, q]
                        if last:
                            p_ref[j, i] = p_new - ratio * g_new
                            g_ref[j, i] = g_new
                        else:
                            p_sum[i] = p_new
                            g_sum[i] = g_new
                h1_before, h2_before = h1, h2

        def per_block(f, _):
            block(f, False)
            return 0

        lax.fori_loop(0, FT - 1, per_block, 0)
        block(FT - 1, True)
        return 0

    lax.fori_loop(0, 15, per_direction, 0)

    numerator(14)
    zero = jnp.zeros((8, 128), jnp.float32)

    def fluxes(rows):
        for k in rows:
            def flux_of(j, totals):
                v_y = dirs[9, pl.ds(first + j, 8, stride=0), :]
                v_z = dirs[10, pl.ds(first + j, 8, stride=0), :]
                place = stored_at(j)
                out = []
                for z, t in cell:
                    flow = g_ref[j, 8 * k + place[z][t]]
                    n = len(out)
                    out += [totals[n] + flow, totals[n + 1] + v_y * flow, totals[n + 2] + v_z * flow]
                return out

            found = lax.fori_loop(0, 15, flux_of, [zero] * 24)
            for n in range(8):
                acc[1, 8 * k + n] = sign * found[3 * n]
                acc[2, 8 * k + n] = found[3 * n + 1]
                acc[3, 8 * k + n] = found[3 * n + 2]

    def summed(which, target, base):
        for z in range(4):
            for t in range(2):
                found = [jnp.sum(acc[which, 8 * k + 2 * z + t], axis=0, keepdims=True) for k in range(4)]
                for x in range(4):
                    at = base + 4 * z + x
                    row = jnp.where(forward, found[x], found[3 - x])
                    target[at : at + 1, t * 128 : (t + 1) * 128] = row

    summed(0, nq, 0)
    moved = permuted(nq[...], w_num[...])
    n_recv[0] = moved[:, 0:128]
    for j in range(1, n_modes):
        n_send[j - 1] = moved[:, j * 128 : (j + 1) * 128]
    n_copies = [
        remote(n_send.at[j - 1], n_recv.at[j], ns.at[j - 1], nr.at[j - 1], (peer(j), s))
        for j in range(1, n_modes)
    ]
    for copy in window_copies():
        copy.wait_recv()
    for b in range(2 * REACH + 1):
        for z in range(4):
            field[z, 4 * b : 4 * b + 4, :] = l_recv[b, 4 * z : 4 * z + 4, :]
    rows = 4 * (2 * REACH + 1)
    padded = rows + 4
    for z in range(4):
        field[z, rows:padded, :] = jnp.zeros((4, 128), jnp.float32)
    x_of = iota((padded, 128), 0) + 4 * (s - REACH)
    y_of_lane = iota((padded, 128), 1) + y0
    inside = (
        (x_of >= 0) & (x_of < 4 * n_space) & (iota((padded, 128), 0) < rows)
        & (y_of_lane >= 0) & (y_of_lane < 256)
    )

    def by_kind(label, base):
        return jnp.where(label == 0.0, tables[base], jnp.where(label == 1.0, tables[base + 1], tables[base + 2]))

    kappa = [jnp.where(inside, by_kind(field[z], 3), 0.0) for z in range(4)]

    def link(here, there):
        mean = 0.5 * (here + there)
        return jnp.where(here > 0.0, mean, 0.0), jnp.where((here > 0.0) & (there > 0.0), mean, 0.0)

    for z in range(4):
        here = kappa[z]
        none = jnp.zeros_like(here)
        around = [
            pltpu.roll(here, 1, 0), pltpu.roll(here, padded - 1, 0),
            pltpu.roll(here, 1, 1), pltpu.roll(here, 127, 1),
            kappa[z - 1] if z > 0 else none, kappa[z + 1] if z < 3 else none,
        ]
        diagonal = jnp.full_like(here, 1.0)
        for which, there in enumerate(around):
            whole, joint = link(here, there)
            diagonal = diagonal + whole
            coup[which, z] = joint
        coup[6, z] = diagonal

    top = 1.0 + 12.0 * jnp.maximum(jnp.maximum(tables[3], tables[4]), tables[5])
    theta = (top + 1.0) / 2.0
    delta = (top - 1.0) / 2.0
    sigma = theta / delta
    rho = 1.0 / sigma
    for k in range(CHEB - 1):
        rho_new = 1.0 / (2.0 * sigma - rho)
        cheb_c[k] = rho_new * rho
        cheb_c[CHEB + k] = 2.0 * rho_new / delta
        rho = rho_new

    fluxes(range(2))
    for copy in n_copies:
        copy.wait_recv()
    numer = (n_recv[0] + n_recv[1]) + (n_recv[2] + n_recv[3])
    here = l_recv[REACH]
    half = numer / (float(ORDINATES) * by_kind(here, 0))
    mismatch = half - t_win[...]
    half_ref[...] = half
    r_send[...] = mismatch
    r_recv[REACH] = mismatch
    r_copies = [
        remote(r_send, r_recv.at[REACH - o], rs.at[i], rr.at[i], (m, beside(o)))
        for i, o in reversed(tuple(enumerate(OFFSETS)))
    ]

    fluxes(range(2, 4))
    for i in range(3):
        summed(1 + i, fq, 16 * i)
    moved = permuted(fq[...], w_flux[...])
    for j in range(n_modes):
        part = moved[:, j * 128 : (j + 1) * 128]
        packed = part[0:24] + pltpu.roll(part[24:48], 64, 1)
        if j == 0:
            f_recv[0] = packed
        else:
            f_send[j - 1] = packed
    f_copies = [
        remote(f_send.at[j - 1], f_recv.at[j], fs.at[j - 1], fr.at[j - 1], (peer(j), s))
        for j in range(1, n_modes)
    ]

    for copy in r_copies:
        copy.wait_recv()
    for b in range(2 * REACH + 1):
        for z in range(4):
            field[z, 4 * b : 4 * b + 4, :] = r_recv[b, 4 * z : 4 * z + 4, :]
    mid = 4 * REACH
    start_r = [jnp.where(inside, field[z], 0.0) for z in range(4)]
    start_d = [r / theta for r in start_r]
    start_c = [d[mid : mid + 8] for d in start_d]

    def advancing(low, high):
        count = high - low

        def advance(k, carry):
            resid, direction, total = carry
            c_1, c_2 = cheb_c[k], cheb_c[CHEB + k]
            new_r, new_d, new_t = [], [], []
            for z in range(4):
                d = direction[z]
                applied = coup[6, z, low:high, :] * d
                applied = applied - coup[0, z, low:high, :] * pltpu.roll(d, 1, 0)
                applied = applied - coup[1, z, low:high, :] * pltpu.roll(d, count - 1, 0)
                applied = applied - coup[2, z, low:high, :] * pltpu.roll(d, 1, 1)
                applied = applied - coup[3, z, low:high, :] * pltpu.roll(d, 127, 1)
                if z > 0:
                    applied = applied - coup[4, z, low:high, :] * direction[z - 1]
                if z < 3:
                    applied = applied - coup[5, z, low:high, :] * direction[z + 1]
                r = resid[z] - applied
                after = c_1 * d + c_2 * r
                new_r.append(r)
                new_d.append(after)
                new_t.append(total[z] + after[mid - low : mid - low + 8])
            return new_r, new_d, new_t

        return advance

    full = CHEB - 1 - 8
    start = lax.fori_loop(0, full, advancing(0, padded), (start_r, start_d, start_c))
    low, high = mid - 8, mid + 16
    start = ([r[low:high] for r in start[0]], [d[low:high] for d in start[1]], start[2])
    _, _, correction = lax.fori_loop(full, CHEB - 1, advancing(low, high), start)
    for z in range(4):
        whole = half_ref[4 * z : 4 * z + 4, :] + correction[z][0:4]
        out_t[z] = pltpu.roll(whole, 96, 1)[:, 0:64]

    for copy in f_copies:
        copy.wait_recv()
    flux = ((f_recv[0] + f_recv[1]) + (f_recv[2] + f_recv[3])) / float(ORDINATES)
    for i in range(3):
        for z in range(4):
            at = 16 * i + 4 * z
            out_f[i, z] = flux[at : at + 4, 0:64] if at < 24 else flux[at - 24 : at - 20, 64:128]

    for copy in halo_copies + look_copies + window_copies() + n_copies + f_copies + r_copies:
        copy.wait_send()


def solution(mesh):
    n_space, n_modes = mesh.shape["space"], mesh.shape["modes"]
    f32, i32 = jnp.float32, jnp.int32
    vmem = pl.BlockSpec(memory_space=pltpu.VMEM)
    dma = pltpu.SemaphoreType.DMA
    blocks = 2 * REACH + 1
    padded = 4 * blocks + 4

    def on_device(temp, source, label, lookup, vel, heat, rates, polar, azimuth):
        scratch = [
            pltpu.VMEM((4, 4, 256), f32), pltpu.VMEM((4, 4, 256), f32), pltpu.VMEM((4, 4, 256), i32),
            pltpu.VMEM((4, 1, 128), i32),
            pltpu.VMEM((80, 256), f32), pltpu.VMEM((80, 256), f32),
            pltpu.VMEM((11, 40, 128), f32), pltpu.VMEM((4, 3, 2, 24, 128), f32), pltpu.VMEM((2, 24 + 8, 128), f32),
            pltpu.VMEM((4, FT, 80, 8, 128), f32), pltpu.VMEM((4, 48, 8, 128), i32),
            pltpu.VMEM((FT, 48, 8, 128), f32), pltpu.VMEM((32, 8, 128), f32), pltpu.VMEM((32, 8, 128), f32),
            pltpu.VMEM((3 * FT, 8, 128), f32), pltpu.VMEM((FT, 8, 128), f32),
            pltpu.VMEM((16, 32, 8, 128), f32), pltpu.VMEM((15, 32, 8, 128), f32),
            pltpu.VMEM((4, 32, 8, 128), f32),
            pltpu.VMEM((256, 256), jnp.bfloat16),
            pltpu.VMEM((256, 128 * n_modes), jnp.bfloat16), pltpu.VMEM((256, 128 * n_modes), jnp.bfloat16),
            pltpu.VMEM((6, 1, 128), f32),
            pltpu.VMEM((16, 128), f32), pltpu.VMEM((16, 128), f32), pltpu.VMEM((blocks, 16, 128), f32),
            pltpu.VMEM((16, 256), f32), pltpu.VMEM((n_modes - 1, 16, 128), f32), pltpu.VMEM((n_modes, 16, 128), f32),
            pltpu.VMEM((48, 256), f32), pltpu.VMEM((n_modes - 1, 24, 128), f32), pltpu.VMEM((n_modes, 24, 128), f32),
            pltpu.VMEM((16, 128), f32), pltpu.VMEM((16, 128), f32), pltpu.VMEM((blocks, 16, 128), f32),
            pltpu.VMEM((4, padded, 128), f32), pltpu.VMEM((7, 4, padded, 128), f32),
            pltpu.VMEM((2 * CHEB, 1, 128), f32),
            pltpu.SemaphoreType.REGULAR((2, 3)),
            dma((3,)), dma((3,)), dma((n_modes - 1,)), dma((n_modes - 1,)),
            dma((2 * REACH,)), dma((2 * REACH,)), dma((n_modes - 1,)), dma((n_modes - 1,)),
            dma((n_modes - 1,)), dma((n_modes - 1,)), dma((2 * REACH,)), dma((2 * REACH,)),
        ]
        call = pl.pallas_call(
            functools.partial(kernel, n_space, n_modes),
            out_shape=(
                pltpu.VMEM((4, 4, 64), f32),
                pltpu.VMEM((3, 4, 4, 64), f32),
            ),
            in_specs=[vmem] * 9 + [pl.BlockSpec(memory_space=pltpu.SMEM)],
            out_specs=(vmem, vmem),
            scratch_shapes=scratch,
            compiler_params=pltpu.CompilerParams(collective_id=0, has_side_effects=True),
        )
        return call(
            temp, source, label, lookup[None], vel[None], heat[None], rates.T,
            polar[None], azimuth[None], azimuth,
        )

    rows = P(None, "space", None)
    return jax.shard_map(
        on_device,
        mesh=mesh,
        in_specs=(rows, rows, rows, P("modes"), P(), P(), P(), P(), P()),
        out_specs=(P(None, "space", "modes"), P(None, None, "space", "modes")),
        check_vma=False,
    )
```

```python
import functools

import jax
import jax.numpy as jnp
from jax import lax
from jax.experimental import pallas as pl
from jax.experimental.pallas import tpu as pltpu
from jax.sharding import PartitionSpec as P

SPECTRAL_BINS = 40
ORDINATES = 60
CHEB = 16
FT = SPECTRAL_BINS // 8
REACH = 4
HALF_PI = 1.5707964
MESH = pl.DeviceIdType.MESH
OFFSETS = tuple(o for r in range(1, REACH + 1) for o in (r, -r))


def iota(shape, dim):
    return lax.broadcasted_iota(jnp.int32, shape, dim)


def permuted(x, chosen):
    rows = x.shape[0]
    first = x.astype(jnp.bfloat16)
    rest = x - first.astype(jnp.float32)
    second = rest.astype(jnp.bfloat16)
    third = (rest - second.astype(jnp.float32)).astype(jnp.bfloat16)
    stacked = jnp.concatenate([first, second, third], axis=0)
    out = jnp.dot(stacked, chosen, preferred_element_type=jnp.float32)
    return out[:rows] + (out[rows : 2 * rows] + out[2 * rows :])


def lookup(table, kind):
    return jnp.take_along_axis(
        table, kind, axis=1, mode="promise_in_bounds", wrap_negative_indices=False
    )


def ones_where(cond):
    return jnp.where(cond, 1.0, 0.0).astype(jnp.bfloat16)


def kernel(
    n_space, n_modes,
    t_ref, s_ref, l_ref, idx_ref, vel_ref, heat_ref, rates_ref, pol_ref, azi_ref, azs_ref,
    out_t, out_f,
    h_t, h_s, h_l, look, raw, il, dirs, wind, d_ref, cells, lab, inv_ref, p_sum, g_sum, q_of, cv, p_ref, g_ref, acc,
    w_int, w_num, w_flux, tables, t_win, l_send, l_recv, nq, n_send, n_recv, fq, f_send, f_recv,
    half_ref, r_send, r_recv, field, coup, cheb_c,
    tokens, hs, hr, ls, lr, ws, wr, ns, nr, fs, fr, rs, rr,
):
    m = lax.axis_index("modes")
    s = lax.axis_index("space")
    forward = m < n_modes // 2
    step = jnp.where(forward, 1, -1)

    def peer(j):
        return lax.rem(m + j, n_modes)

    def beside(o):
        return lax.rem(s + o + n_space, n_space)

    barrier = pltpu.get_barrier_semaphore()
    for j in range(1, n_modes):
        pl.semaphore_signal(barrier, inc=1, device_id=(peer(j), s), device_id_type=MESH)
    for o in (1, -1):
        pl.semaphore_signal(barrier, inc=1, device_id=(m, beside(o)), device_id_type=MESH)

    y0 = 64 * m - 32
    natural = ones_where(iota((256, 128), 0) == iota((256, 128), 1) + y0)
    for z in range(4):
        raw[pl.ds(4 * z, 4), :] = t_ref[z]
        raw[pl.ds(16 + 4 * z, 4), :] = l_ref[z].astype(jnp.float32)
    windows = permuted(raw[0:32, :], natural)
    t_win[...] = windows[0:16]
    l_send[...] = windows[16:32]
    l_recv[REACH] = windows[16:32]
    look[0] = jnp.zeros((1, 128), jnp.int32)
    look[0, :, 0:10] = idx_ref[...]

    spot = iota((32, 128), 0) == iota((32, 128), 1)

    def column(row_ref):
        row = jnp.concatenate([row_ref[...], jnp.zeros((1, 98), jnp.float32)], axis=1)
        picked = jnp.where(spot, jnp.broadcast_to(row, (32, 128)), 0.0)
        return jnp.broadcast_to(jnp.sum(picked, axis=1, keepdims=True), (32, 128))

    polar, azimuth = column(pol_ref), column(azi_ref)
    sign = jnp.where(forward, 1.0, -1.0)
    u_x = jnp.cos(polar)
    u_y = jnp.sin(polar) * jnp.cos(azimuth)
    u_z = jnp.sin(polar) * jnp.sin(azimuth)
    y_up = jnp.where(jnp.abs(azimuth) < HALF_PI, sign, -sign)
    z_up = jnp.where(azimuth > 0.0, sign, -sign)
    dirs[0, 0:32, :] = u_x
    dirs[1, 0:32, :] = jnp.abs(u_y)
    dirs[2, 0:32, :] = jnp.abs(u_z)
    dirs[3, 0:32, :] = u_x + jnp.abs(u_y) + jnp.abs(u_z)
    dirs[4, 0:32, :] = y_up
    dirs[5, 0:32, :] = z_up
    dirs[6, 0:32, :] = jnp.abs(u_y) / u_x
    dirs[7, 0:32, :] = jnp.abs(u_z) / u_x
    dirs[8, 0:32, :] = (u_x + jnp.abs(u_y) + jnp.abs(u_z)) / u_x
    dirs[9, 0:32, :] = sign * u_y / u_x
    dirs[10, 0:32, :] = sign * u_z / u_x

    y_of = 2 * (iota((256, 128), 0) & 127) + (iota((256, 128), 0) >> 7)
    lane = iota((256, 128), 1)
    for tile in range(2):
        w_int[:, tile * 128 : (tile + 1) * 128] = ones_where(iota((256, 128), 0) == 2 * lane + tile)
    for j in range(n_modes):
        w_num[:, j * 128 : (j + 1) * 128] = ones_where(y_of == lane + (64 * peer(j) - 32))
        w_flux[:, j * 128 : (j + 1) * 128] = ones_where((y_of == lane + 64 * peer(j)) & (lane < 64))

    pl.semaphore_wait(barrier, n_modes + 1)

    def described(source, target, send, recv, device):
        return pltpu.make_async_remote_copy(
            src_ref=source, dst_ref=target, send_sem=send, recv_sem=recv,
            device_id=device, device_id_type=MESH,
        )

    def remote(*of):
        copy = described(*of)
        copy.start()
        return copy

    def tell(level):
        for side in range(2):
            pl.semaphore_signal(
                tokens.at[side, level], inc=1, device_id=(m, beside(1 - 2 * side)), device_id_type=MESH
            )

    def hear(level):
        for side in range(2):
            pl.semaphore_wait(tokens.at[side, level], 1)

    down = (m, beside(step))
    halo_copies = [
        remote(t_ref, h_t, hs.at[0], hr.at[0], down),
        remote(s_ref, h_s, hs.at[1], hr.at[1], down),
        remote(l_ref, h_l, hs.at[2], hr.at[2], down),
    ]
    look_copies = [
        remote(look.at[0], look.at[j], ls.at[j - 1], lr.at[j - 1], (peer(j), s))
        for j in range(1, n_modes)
    ]
    tell(0)

    def window_copies():
        return [
            described(l_send, l_recv.at[REACH - o], ws.at[i], wr.at[i], (m, beside(o)))
            for i, o in enumerate(OFFSETS)
        ]

    for copy in look_copies:
        copy.wait_recv()
    freq = iota((SPECTRAL_BINS, 128), 0)
    slot = freq // 10
    spread = jnp.zeros((SPECTRAL_BINS, 128), jnp.float32)
    ordinal = jnp.zeros((SPECTRAL_BINS, 128), jnp.float32)
    for j in range(n_modes):
        row = jnp.broadcast_to(look[j].astype(jnp.float32), (SPECTRAL_BINS, 128))
        spread = jnp.where(slot == j, row, spread)
        owner = lax.rem(m + n_modes - j, n_modes)
        ordinal = jnp.where(slot == j, (10 * owner + 1).astype(jnp.float32), ordinal)
    within = freq - 10 * slot
    spectral = (ordinal + within.astype(jnp.float32)) / float(SPECTRAL_BINS)
    index = jnp.sum(
        jnp.where(iota((SPECTRAL_BINS, 128), 1) == within, spread, 0.0), axis=1, keepdims=True
    )
    chosen = iota((SPECTRAL_BINS, 64), 1).astype(jnp.float32) == index
    onehot = jnp.where(chosen, 1.0, 0.0)

    def looked_up(row):
        found = jnp.sum(onehot * row, axis=1, keepdims=True)
        return jnp.broadcast_to(found, (SPECTRAL_BINS, 128))

    velocity = looked_up(vel_ref[...])
    capacity = looked_up(heat_ref[...]) * spectral
    by_kind_of_f = [looked_up(rates_ref[k : k + 1, :]) for k in range(3)]
    kind_lane = lax.rem(iota((SPECTRAL_BINS, 128), 1), 3)
    rate = jnp.where(kind_lane == 0, by_kind_of_f[0], jnp.where(kind_lane == 1, by_kind_of_f[1], by_kind_of_f[2]))
    kinds = iota((1, 128), 1)
    rate_total = jnp.sum(capacity * rate, axis=0, keepdims=True)
    cond = capacity * velocity * velocity / (3.0 * rate)
    cond_total = jnp.sum(cond, axis=0, keepdims=True)
    conduct = cond_total / rate_total
    for k in range(3):
        def splat(row):
            one = jnp.sum(jnp.where(kinds == k, row, 0.0), axis=1, keepdims=True)
            return jnp.broadcast_to(one, (1, 128))
        tables[k] = splat(rate_total)
        tables[3 + k] = splat(conduct)
    cap_v = capacity * velocity
    inv_v = 1.0 / velocity
    for f in range(FT):
        for kind in range(3):
            q_of[3 * f + kind] = (by_kind_of_f[kind] / velocity)[8 * f : 8 * f + 8]
        cv[f] = cap_v[8 * f : 8 * f + 8]

    def row_of(ref, base, z):
        return jnp.where(forward, ref[z, base : base + 1, :], ref[z, 3 - base : 4 - base, :])

    def fill_cells(i):
        k, z = i // 4, i % 4
        for tile in range(2):
            cols = slice(tile * 128, (tile + 1) * 128)
            kind = jnp.broadcast_to(il[56 + i : 57 + i, cols], (8, 128)).astype(jnp.int32)
            is_0, is_1 = kind == 0, kind == 1
            temp = jnp.broadcast_to(il[4 + i : 5 + i, cols], (8, 128))
            heat = jnp.broadcast_to(il[32 + i : 33 + i, cols], (8, 128))
            spots = [(2 * a + b, 8 * k + 2 * abs(3 * a - z) + abs(b - tile)) for a in range(2) for b in range(2)]
            for order, at in spots:
                lab[order, at] = kind
            for f in range(FT):
                q = jnp.where(is_0, q_of[3 * f], jnp.where(is_1, q_of[3 * f + 1], q_of[3 * f + 2]))
                value = q * temp + inv_v[8 * f : 8 * f + 8] * heat
                for order, at in spots:
                    cells[order, f, at] = value
                if k >= 2:
                    value = cv[f] * value
                    for order, at in spots:
                        cells[order, f, 32 + at] = value

    for k in range(4):
        for z in range(4):
            at = 4 * k + z
            raw[at : at + 1, :] = row_of(t_ref, k, z)
            raw[16 + at : 17 + at, :] = row_of(s_ref, k, z)
            raw[32 + at : 33 + at, :] = row_of(l_ref, k, z).astype(jnp.float32)
    turned = permuted(raw[0:48, :], w_int[...])
    il[12:28, :] = turned[0:16]
    il[40:56, :] = turned[16:32]
    il[64:80, :] = turned[32:48]
    il[28:32, :] = jnp.zeros((4, 256), jnp.float32)
    for i in range(8, 24):
        fill_cells(i)

    for copy in halo_copies:
        copy.wait_recv()
    has = jnp.where(forward, s > 0, s < n_space - 1)
    raw[28:32, :] = jnp.zeros((4, 256), jnp.float32)
    for k in range(3):
        for z in range(4):
            at = 4 * k + z
            raw[at : at + 1, :] = jnp.where(has, row_of(h_t, k + 1, z), 0.0)
            if k > 0:
                raw[8 + at : 9 + at, :] = jnp.where(has, row_of(h_s, k + 1, z), 0.0)
                raw[16 + at : 17 + at, :] = row_of(h_l, k + 1, z).astype(jnp.float32)
    turned = permuted(raw[0:32, :], w_int[...])
    il[0:12, :] = turned[0:12]
    il[32:40, :] = turned[12:20]
    il[56:64, :] = turned[20:28]
    for i in range(8):
        fill_cells(i)

    for k in range(7):
        for z in range(4):
            at = 4 * k + z
            raw[at : at + 1, :] = il[4 * k + 3 - z : 4 * k + 4 - z, :]
    level = iota((24, 128), 0) & 3
    tile_lane = iota((24, 128), 1)
    for a, rows in enumerate((il, raw)):
        for b in range(2):
            near = [slice(0, 128), slice(128, 256)] if b == 0 else [slice(128, 256), slice(0, 128)]
            for q in range(2):
                wind[2 * a + b, 0, q] = rows[0:24, near[q]]
                wind[2 * a + b, 2, q] = jnp.where(level == 0, 0.0, rows[3:27, near[q]])
            edge, turn = (0, 1) if b == 0 else (127, 127)
            wind[2 * a + b, 1, 0] = jnp.where(tile_lane == edge, 0.0, pltpu.roll(rows[4:28, near[1]], turn, 1))
            wind[2 * a + b, 1, 1] = rows[4:28, near[0]]

    lanes8 = iota((8, 128), 1)
    first = lax.rem(m, n_modes // 2) * 15

    def upwind_order(j):
        angle = azs_ref[first + j]
        ahead = jnp.logical_xor(jnp.abs(angle) < HALF_PI, jnp.logical_not(forward))
        up = jnp.logical_xor(angle > 0.0, jnp.logical_not(forward))
        return up, ahead

    both = range(2)
    cell = [(z, q) for z in range(4) for q in both]

    def stored_at(j):
        up, ahead = upwind_order(j)
        levels = [jnp.where(up, z, 3 - z) for z in range(4)]
        tiles = [jnp.where(ahead, q, 1 - q) for q in both]
        return [[2 * levels[z] + tiles[t] for t in both] for z in range(4)]

    def numerator(j):
        place = stored_at(jnp.maximum(j, 0))
        held = jnp.where(j < 0, 15, j)
        for k in range(4):
            for z, t in cell:
                acc[0, 8 * k + 2 * z + t] += p_ref[held, 8 * k + place[z][t]]

    for i in range(32):
        acc[0, i] = jnp.zeros((8, 128), jnp.float32)
        p_ref[15, i] = jnp.zeros((8, 128), jnp.float32)
    hear(0)
    tell(1)

    def per_direction(j, _):
        @pl.when(j == 3)
        def _():
            hear(1)
            tell(2)

        @pl.when(j == 6)
        def _():
            hear(2)
            for copy in window_copies():
                copy.start()

        numerator(j - 1)

        def coef(which):
            return dirs[which, pl.ds(first + j, 8, stride=0), :]

        def tall(row):
            return jnp.concatenate([row] * 3, axis=0)

        up, ahead = upwind_order(j)
        order = jnp.where(up, 0, 2) + jnp.where(ahead, 0, 1)
        turn = jnp.where(ahead, 1, 127)
        a_x, a_y, a_z, a_sum = tall(coef(0)), tall(coef(1)), tall(coef(2)), coef(3)
        for q in both:
            d_ref[q, 0:24, :] = a_x * wind[order, 0, q] + (a_y * wind[order, 1, q] + a_z * wind[order, 2, q])
        r_y, r_z, ratio = coef(6), coef(7), coef(8)
        r_edge = jnp.where(lanes8 == jnp.where(ahead, 0, 127), 0.0, r_y)
        slope = coef(0)
        weights = [[slope / (a_sum + q_of[3 * f + kind]) for kind in range(3)] for f in range(FT)]
        for at in range(48):
            kind = lab[order, at]
            is_0, is_1 = kind == 0, kind == 1
            for f in range(FT):
                w = weights[f]
                inv_ref[f, at] = jnp.where(is_0, w[0], jnp.where(is_1, w[1], w[2]))
        def block(f, begun, last):
            scaled = (cv[f], cv[f] * r_y, cv[f] * r_edge, cv[f] * r_z)
            h1_before = h2_before = None

            def gathered(before, now, scale, source):
                c_x, c_y, c_edge, c_z = scale
                out = {}
                for z in range(4):
                    along = (c_edge * pltpu.roll(now[z, 1], turn, 1), c_y * now[z, 0])
                    for q in both:
                        behind = before[z, q] if c_x is None else c_x * before[z, q]
                        total = (behind + along[q]) + source(2 * z + q)
                        out[z, q] = total + c_z * now[z - 1, q] if z > 0 else total
                return out

            for k in range(6):
                inv = {(z, q): inv_ref[f, 8 * k + 2 * z + q] for z, q in cell}
                here = {(z, q): cells[order, f, 8 * k + 2 * z + q] for z, q in cell}
                h1 = {
                    (z, q): inv[z, q] * (d_ref[q, pl.ds(4 * k + z, 8, stride=0), :] + here[z, q])
                    for z, q in cell
                }
                h2 = None
                if k >= 1:
                    total = gathered(h1_before, h1, (None, r_y, r_edge, r_z), lambda i: here[i // 2, i % 2])
                    h2 = {c: inv[c] * total[c] for c in cell}
                if k >= 2:
                    total = gathered(h2_before, h2, scaled, lambda i: cells[order, f, 32 + 8 * k + i])
                    for z, q in cell:
                        i = 8 * (k - 2) + 2 * z + q
                        p_new, g_new = total[z, q], inv[z, q] * total[z, q]
                        if begun:
                            p_new, g_new = p_sum[i] + p_new, g_sum[i] + g_new
                        if last:
                            p_ref[j, i] = p_new - ratio * g_new
                            g_ref[j, i] = g_new
                        else:
                            p_sum[i] = p_new
                            g_sum[i] = g_new
                h1_before, h2_before = h1, h2

        def per_block(f, _):
            block(f, True, False)
            return 0

        block(0, False, False)
        lax.fori_loop(1, FT - 1, per_block, 0)
        block(FT - 1, True, True)
        return 0

    lax.fori_loop(0, 15, per_direction, 0)

    numerator(14)
    zero = jnp.zeros((8, 128), jnp.float32)

    def fluxes(rows):
        for k in rows:
            def flux_of(j, totals):
                v_y = dirs[9, pl.ds(first + j, 8, stride=0), :]
                v_z = dirs[10, pl.ds(first + j, 8, stride=0), :]
                place = stored_at(j)
                out = []
                for z, t in cell:
                    flow = g_ref[j, 8 * k + place[z][t]]
                    n = len(out)
                    out += [totals[n] + flow, totals[n + 1] + v_y * flow, totals[n + 2] + v_z * flow]
                return out

            found = lax.fori_loop(0, 15, flux_of, [zero] * 24)
            for n in range(8):
                acc[1, 8 * k + n] = sign * found[3 * n]
                acc[2, 8 * k + n] = found[3 * n + 1]
                acc[3, 8 * k + n] = found[3 * n + 2]

    def summed(which, target, base):
        for z in range(4):
            for t in range(2):
                found = [jnp.sum(acc[which, 8 * k + 2 * z + t], axis=0, keepdims=True) for k in range(4)]
                for x in range(4):
                    at = base + 4 * z + x
                    row = jnp.where(forward, found[x], found[3 - x])
                    target[at : at + 1, t * 128 : (t + 1) * 128] = row

    summed(0, nq, 0)
    moved = permuted(nq[...], w_num[...])
    n_recv[0] = moved[:, 0:128]
    for j in range(1, n_modes):
        n_send[j - 1] = moved[:, j * 128 : (j + 1) * 128]
    n_copies = [
        remote(n_send.at[j - 1], n_recv.at[j], ns.at[j - 1], nr.at[j - 1], (peer(j), s))
        for j in range(1, n_modes)
    ]
    for copy in window_copies():
        copy.wait_recv()
    for b in range(2 * REACH + 1):
        for z in range(4):
            field[z, 4 * b : 4 * b + 4, :] = l_recv[b, 4 * z : 4 * z + 4, :]
    rows = 4 * (2 * REACH + 1)
    padded = rows + 4
    for z in range(4):
        field[z, rows:padded, :] = jnp.zeros((4, 128), jnp.float32)
    x_of = iota((padded, 128), 0) + 4 * (s - REACH)
    y_of_lane = iota((padded, 128), 1) + y0
    inside = (
        (x_of >= 0) & (x_of < 4 * n_space) & (iota((padded, 128), 0) < rows)
        & (y_of_lane >= 0) & (y_of_lane < 256)
    )

    def by_kind(label, base):
        return jnp.where(label == 0.0, tables[base], jnp.where(label == 1.0, tables[base + 1], tables[base + 2]))

    kappa = [jnp.where(inside, by_kind(field[z], 3), 0.0) for z in range(4)]

    def link(here, there):
        mean = 0.5 * (here + there)
        return jnp.where(here > 0.0, mean, 0.0), jnp.where((here > 0.0) & (there > 0.0), mean, 0.0)

    for z in range(4):
        here = kappa[z]
        none = jnp.zeros_like(here)
        around = [
            pltpu.roll(here, 1, 0), pltpu.roll(here, padded - 1, 0),
            pltpu.roll(here, 1, 1), pltpu.roll(here, 127, 1),
            kappa[z - 1] if z > 0 else none, kappa[z + 1] if z < 3 else none,
        ]
        diagonal = jnp.full_like(here, 1.0)
        for which, there in enumerate(around):
            whole, joint = link(here, there)
            diagonal = diagonal + whole
            coup[which, z] = joint
        coup[6, z] = diagonal

    top = 1.0 + 12.0 * jnp.maximum(jnp.maximum(tables[3], tables[4]), tables[5])
    theta = (top + 1.0) / 2.0
    delta = (top - 1.0) / 2.0
    sigma = theta / delta
    rho = 1.0 / sigma
    for k in range(CHEB - 1):
        rho_new = 1.0 / (2.0 * sigma - rho)
        cheb_c[k] = rho_new * rho
        cheb_c[CHEB + k] = 2.0 * rho_new / delta
        rho = rho_new

    fluxes(range(2))
    for copy in n_copies:
        copy.wait_recv()
    numer = (n_recv[0] + n_recv[1]) + (n_recv[2] + n_recv[3])
    here = l_recv[REACH]
    half = numer / (float(ORDINATES) * by_kind(here, 0))
    mismatch = half - t_win[...]
    half_ref[...] = half
    r_send[...] = mismatch
    r_recv[REACH] = mismatch
    r_copies = [
        remote(r_send, r_recv.at[REACH - o], rs.at[i], rr.at[i], (m, beside(o)))
        for i, o in reversed(tuple(enumerate(OFFSETS)))
    ]

    fluxes(range(2, 4))
    for i in range(3):
        summed(1 + i, fq, 16 * i)
    moved = permuted(fq[...], w_flux[...])
    for j in range(n_modes):
        part = moved[:, j * 128 : (j + 1) * 128]
        packed = part[0:24] + pltpu.roll(part[24:48], 64, 1)
        if j == 0:
            f_recv[0] = packed
        else:
            f_send[j - 1] = packed
    f_copies = [
        remote(f_send.at[j - 1], f_recv.at[j], fs.at[j - 1], fr.at[j - 1], (peer(j), s))
        for j in range(1, n_modes)
    ]

    for copy in r_copies:
        copy.wait_recv()
    for b in range(2 * REACH + 1):
        for z in range(4):
            field[z, 4 * b : 4 * b + 4, :] = r_recv[b, 4 * z : 4 * z + 4, :]
    mid = 4 * REACH
    start_r = [jnp.where(inside, field[z], 0.0) for z in range(4)]
    start_d = [r / theta for r in start_r]
    start_c = [d[mid : mid + 8] for d in start_d]

    def advancing(low, high):
        count = high - low

        def advance(k, carry):
            resid, direction, total = carry
            c_1, c_2 = cheb_c[k], cheb_c[CHEB + k]
            new_r, new_d, new_t = [], [], []
            for z in range(4):
                d = direction[z]
                applied = coup[6, z, low:high, :] * d
                applied = applied - coup[0, z, low:high, :] * pltpu.roll(d, 1, 0)
                applied = applied - coup[1, z, low:high, :] * pltpu.roll(d, count - 1, 0)
                applied = applied - coup[2, z, low:high, :] * pltpu.roll(d, 1, 1)
                applied = applied - coup[3, z, low:high, :] * pltpu.roll(d, 127, 1)
                if z > 0:
                    applied = applied - coup[4, z, low:high, :] * direction[z - 1]
                if z < 3:
                    applied = applied - coup[5, z, low:high, :] * direction[z + 1]
                r = resid[z] - applied
                after = c_1 * d + c_2 * r
                new_r.append(r)
                new_d.append(after)
                new_t.append(total[z] + after[mid - low : mid - low + 8])
            return new_r, new_d, new_t

        return advance

    full = CHEB - 1 - 8
    start = lax.fori_loop(0, full, advancing(0, padded), (start_r, start_d, start_c))
    low, high = mid - 8, mid + 16
    start = ([r[low:high] for r in start[0]], [d[low:high] for d in start[1]], start[2])
    _, _, correction = lax.fori_loop(full, CHEB - 1, advancing(low, high), start)
    for z in range(4):
        whole = half_ref[4 * z : 4 * z + 4, :] + correction[z][0:4]
        out_t[z] = pltpu.roll(whole, 96, 1)[:, 0:64]

    for copy in f_copies:
        copy.wait_recv()
    flux = ((f_recv[0] + f_recv[1]) + (f_recv[2] + f_recv[3])) / float(ORDINATES)
    for i in range(3):
        for z in range(4):
            at = 16 * i + 4 * z
            out_f[i, z] = flux[at : at + 4, 0:64] if at < 24 else flux[at - 24 : at - 20, 64:128]

    for copy in halo_copies + look_copies + window_copies() + n_copies + f_copies + r_copies:
        copy.wait_send()


def solution(mesh):
    n_space, n_modes = mesh.shape["space"], mesh.shape["modes"]
    f32, i32 = jnp.float32, jnp.int32
    vmem = pl.BlockSpec(memory_space=pltpu.VMEM)
    dma = pltpu.SemaphoreType.DMA
    blocks = 2 * REACH + 1
    padded = 4 * blocks + 4

    def on_device(temp, source, label, lookup, vel, heat, rates, polar, azimuth):
        scratch = [
            pltpu.VMEM((4, 4, 256), f32), pltpu.VMEM((4, 4, 256), f32), pltpu.VMEM((4, 4, 256), i32),
            pltpu.VMEM((4, 1, 128), i32),
            pltpu.VMEM((80, 256), f32), pltpu.VMEM((80, 256), f32),
            pltpu.VMEM((11, 40, 128), f32), pltpu.VMEM((4, 3, 2, 24, 128), f32), pltpu.VMEM((2, 24 + 8, 128), f32),
            pltpu.VMEM((4, FT, 80, 8, 128), f32), pltpu.VMEM((4, 48, 8, 128), i32),
            pltpu.VMEM((FT, 48, 8, 128), f32), pltpu.VMEM((32, 8, 128), f32), pltpu.VMEM((32, 8, 128), f32),
            pltpu.VMEM((3 * FT, 8, 128), f32), pltpu.VMEM((FT, 8, 128), f32),
            pltpu.VMEM((16, 32, 8, 128), f32), pltpu.VMEM((15, 32, 8, 128), f32),
            pltpu.VMEM((4, 32, 8, 128), f32),
            pltpu.VMEM((256, 256), jnp.bfloat16),
            pltpu.VMEM((256, 128 * n_modes), jnp.bfloat16), pltpu.VMEM((256, 128 * n_modes), jnp.bfloat16),
            pltpu.VMEM((6, 1, 128), f32),
            pltpu.VMEM((16, 128), f32), pltpu.VMEM((16, 128), f32), pltpu.VMEM((blocks, 16, 128), f32),
            pltpu.VMEM((16, 256), f32), pltpu.VMEM((n_modes - 1, 16, 128), f32), pltpu.VMEM((n_modes, 16, 128), f32),
            pltpu.VMEM((48, 256), f32), pltpu.VMEM((n_modes - 1, 24, 128), f32), pltpu.VMEM((n_modes, 24, 128), f32),
            pltpu.VMEM((16, 128), f32), pltpu.VMEM((16, 128), f32), pltpu.VMEM((blocks, 16, 128), f32),
            pltpu.VMEM((4, padded, 128), f32), pltpu.VMEM((7, 4, padded, 128), f32),
            pltpu.VMEM((2 * CHEB, 1, 128), f32),
            pltpu.SemaphoreType.REGULAR((2, 3)),
            dma((3,)), dma((3,)), dma((n_modes - 1,)), dma((n_modes - 1,)),
            dma((2 * REACH,)), dma((2 * REACH,)), dma((n_modes - 1,)), dma((n_modes - 1,)),
            dma((n_modes - 1,)), dma((n_modes - 1,)), dma((2 * REACH,)), dma((2 * REACH,)),
        ]
        call = pl.pallas_call(
            functools.partial(kernel, n_space, n_modes),
            out_shape=(
                pltpu.VMEM((4, 4, 64), f32),
                pltpu.VMEM((3, 4, 4, 64), f32),
            ),
            in_specs=[vmem] * 9 + [pl.BlockSpec(memory_space=pltpu.SMEM)],
            out_specs=(vmem, vmem),
            scratch_shapes=scratch,
            compiler_params=pltpu.CompilerParams(collective_id=0, has_side_effects=True),
        )
        return call(
            temp, source, label, lookup[None], vel[None], heat[None], rates.T,
            polar[None], azimuth[None], azimuth,
        )

    rows = P(None, "space", None)
    return jax.shard_map(
        on_device,
        mesh=mesh,
        in_specs=(rows, rows, rows, P("modes"), P(), P(), P(), P(), P()),
        out_specs=(P(None, "space", "modes"), P(None, None, "space", "modes")),
        check_vma=False,
    )
```
